32 devices in a mesh: dp: 8 (over y, x, core), head: 4 (over z).
Axes of the slice: x: 2, y: 2, z: 4, core: 2. Of those that a mesh axis runs over, the one named last changes fastest.
Arguments:
- tokens_in: bfloat16 [16384, 768], P(('dp', 'head')), may hold values from -6 to 6
- gain_attn: float32 [768], replicated, may hold values from 0.1 to 1.9
- gain_ffn: float32 [768], replicated, may hold values from 0.1 to 1.9
- w_qkv: bfloat16 [3, 768, 768], P(None, None, 'head'), may hold values from -0.3125 to 0.3125
- w_out: bfloat16 [768, 768], P('head'), may hold values from -0.5 to 0.5
- w_up: bfloat16 [768, 768], replicated, may hold values from -0.21875 to 0.21875
- w_down: bfloat16 [768, 768], replicated, may hold values from -0.21875 to 0.21875
- slot_mol: int32 [8, 16], P('dp'), may hold values from 0 to 11, never falling along the last dimension, each value on 1 to 2 neighbouring positions
- slot_fill: int32 [8, 16], P('dp'), may hold values from 16 to 128
- cotangent: bfloat16 [16384, 768], P(('dp', 'head')), may hold values from -6 to 6
Outputs:
- layer_out: bfloat16 [16384, 768], P(('dp', 'head'))
- d_tokens: float32 [16384, 768], P(('dp', 'head'))
- d_gain_attn: float32 [768], replicated
- d_gain_ffn: float32 [768], replicated
- d_w_qkv: float32 [3, 768, 768], P(None, None, 'head')
- d_w_out: float32 [768, 768], P('head')
- d_w_up: float32 [768, 768], replicated
- d_w_down: float32 [768, 768], replicated
The draws below stay inside these ranges and needn't reach their ends.
Inputs may be any that keep to these rules, and one draw needn't show every extreme that they name: `slot_mol`: each group holds 12 molecules numbered in slot order; a molecule takes one slot or two consecutive slots. `slot_fill`: the live tokens of a slot are its first rows.
All inputs are finite; a program needn't handle non-finite values.
Results may differ from the reference program's by a relative error of at most 0.015.
The reference program's roundings to bfloat16 on the way count: a program that leaves them out, or rounds other values in their place, can miss the bound.
Values may be sent and summed in bfloat16 or wider, within the bound.
A program may use at most 128 MiB of HBM per device.

```python
import math
import jax
import jax.numpy as jnp
import numpy as np
from jax import lax

D = 768
HEADS = 32
HEAD_DIM = 24
FF = 768
SLOT_LEN = 128
SLOTS = 16
GROUPS = 8
TOKENS = 16384
MOLS = 12


def place_ends(result, key, smallest, top_value):
    longest = result.shape.index(max(result.shape))
    spots = []
    for shift in (0, 1):
        where = [jax.random.randint(jax.random.fold_in(key, axis), (), 0, length) for axis, length in enumerate(result.shape)]
        where[longest] = (where[longest] + shift) % result.shape[longest]
        spots.append(tuple(where))
    return result.at[spots[0]].set(smallest).at[spots[1]].set(top_value)


def shard_levels(stream_key, dims, pieces, least, high):
    level, own = 1.0, jax.random.fold_in(stream_key, 6)
    for axis_at, parts in pieces:
        draws = jnp.exp(jax.random.uniform(jax.random.fold_in(own, axis_at), (parts,), jnp.float32, least / len(pieces), high / len(pieces)))
        level = level * jnp.repeat(draws, dims[axis_at] // parts).reshape([-1 if axis == axis_at else 1 for axis in range(len(dims))])
    return level


def profile(count, total, reach, slope):
    loads = [(1 << 20) // math.isqrt(grade ** slope) + 1 for grade in range(2, count + 1)]
    spare, counts = total - reach - (count - 1), [1] * (count - 1)
    while spare > 0:
        movable = [i for i in range(count - 1) if counts[i] < reach]
        whole, left = sum([loads[i] for i in movable]), spare
        for i in movable:
            more = min(reach - counts[i], max(1, left * loads[i] // whole), spare)
            counts[i] = counts[i] + more
            spare = spare - more
    return np.array([reach] + counts)


def ragged_sizes(key, amount, total, limit, skew):
    if amount == 2:
        one = jax.random.randint(key, (), max(1, total - limit), min(limit, total - 1) + 1)
        return jnp.stack([one, total - one])
    tallies = jnp.asarray(profile(amount, total, limit, skew), jnp.int32)
    couples = (amount - 1) // 2
    source_of, taker = tallies[1:1 + 2 * couples:2], tallies[2:2 + 2 * couples:2]
    slack = jnp.minimum(source_of - 1, limit - taker)
    shifted = jax.random.randint(jax.random.fold_in(key, 1), (couples,), 0, 1 << 20) % (slack + 1)
    tallies = tallies.at[1:1 + 2 * couples:2].set(source_of - shifted).at[2:2 + 2 * couples:2].set(taker + shifted)
    return tallies[jax.random.permutation(jax.random.fold_in(key, 2), amount)]


def normal_values(key, dims, spread, bound, cuts=(), kind=jnp.bfloat16):
    factor_of = shard_levels(key, dims, cuts, -0.22, 0.18) if cuts else 1.0
    entries = jax.random.normal(key, dims, jnp.float32) * spread * factor_of
    return jnp.minimum(jnp.maximum(entries, -bound), bound).astype(kind)


def setup_inputs(seed: int = 0) -> dict:
    arg_keys = jax.random.split(jax.random.key(seed), 11)
    return {
        "tokens_in": normal_values(arg_keys[0], (TOKENS, D), 1.0, 6.0, ((0, 32),)),
        "gain_attn": jnp.clip(1.0 + 0.18 * jax.random.normal(arg_keys[1], (D,), jnp.float32), 0.1, 1.9),
        "gain_ffn": jnp.clip(1.0 + 0.18 * jax.random.normal(arg_keys[2], (D,), jnp.float32), 0.1, 1.9),
        "w_qkv": normal_values(arg_keys[3], (3, D, D), (D // 2) ** -0.5, 0.3125, ((2, 4),)),
        "w_out": normal_values(arg_keys[4], (D, D), 128 ** -0.5, 0.5, ((0, 4),)),
        "w_up": normal_values(arg_keys[5], (D, FF), D ** -0.5, 0.21875),
        "w_down": normal_values(arg_keys[6], (FF, D), FF ** -0.5, 0.21875),
        "slot_mol": jax.vmap(lambda own: jnp.searchsorted(jnp.cumsum(ragged_sizes(own, MOLS, SLOTS, 2, 0)), jnp.arange(SLOTS), side="right"))(jax.random.split(arg_keys[7], GROUPS)).reshape((GROUPS, SLOTS)).astype(jnp.int32),
        "slot_fill": place_ends(jax.random.randint(arg_keys[8], (GROUPS, SLOTS), SLOT_LEN // 8, SLOT_LEN + 1), jax.random.fold_in(arg_keys[8], 1), SLOT_LEN // 8, SLOT_LEN).astype(jnp.int32),
        "cotangent": normal_values(arg_keys[9], (TOKENS, D), 1.0, 6.0, ((0, 32),)),
    }


@jax.custom_vjp
def low(v):
    return lax.optimization_barrier(v.astype(jnp.bfloat16)).astype(jnp.float32)

@jax.custom_vjp
def low_back(v):
    return v

def low_keep(v):
    return (low(v), None)

def low_pass(kept, grad):
    return (grad,)

def back_keep(v):
    return (v, None)

def back_low(kept, grad):
    return (low(grad),)
low.defvjp(low_keep, low_pass)
low_back.defvjp(back_keep, back_low)
epsilon = 1e-05
masked_score = -1000000000.0
highest = lax.Precision.HIGHEST

def layer_norm(values, scale_gain):
    row_mean = lax.optimization_barrier(jnp.mean(values, axis=-1, keepdims=True))
    centred = values - row_mean
    variance = lax.optimization_barrier(jnp.mean(centred * centred, axis=-1, keepdims=True))
    return centred * lax.rsqrt(variance + epsilon) * scale_gain

def group_layer(group_input, mol_rows, live_rows, gain_attn, gain_ffn, w_qkv, w_out, w_up, w_down):
    row_total = group_input.shape[0]
    normed = low(layer_norm(group_input, gain_attn))
    projected = jnp.einsum('td,cde->cte', normed, w_qkv, precision=highest)
    queries = low(HEAD_DIM ** (-0.5) * low_back(projected[0])).reshape(row_total, HEADS, HEAD_DIM)
    keys_all = low(low_back(projected[1])).reshape(row_total, HEADS, HEAD_DIM)
    values_all = low(low_back(projected[2])).reshape(row_total, HEADS, HEAD_DIM)
    block_rows = min(512, row_total)
    block_count = row_total // block_rows

    def attend(block_index):
        first_row = block_index * block_rows
        query_block = lax.dynamic_slice_in_dim(queries, first_row, block_rows, 0)
        mol_block = lax.dynamic_slice_in_dim(mol_rows, first_row, block_rows, 0)
        scores = low_back(jnp.einsum('qhe,khe->hqk', query_block, keys_all, precision=highest))
        allowed = (mol_block[:, None] == mol_rows[None, :]) & live_rows[None, :]
        scores = jnp.where(allowed[None], scores, masked_score)
        attn_probs = low(jax.nn.softmax(scores, axis=-1))
        mixed_block = jnp.einsum('hqk,khe->qhe', attn_probs, values_all, precision=highest)
        return mixed_block.reshape(block_rows, D)
    mixed_heads = lax.map(jax.checkpoint(attend), jnp.arange(block_count, dtype=jnp.int32))
    mixed_heads = low(low_back(mixed_heads.reshape(row_total, D)))
    residual = group_input + low_back(jnp.dot(mixed_heads, w_out, precision=highest))
    normed_ffn = low(layer_norm(residual, gain_ffn))
    ffn_inner = low_back(jnp.dot(normed_ffn, w_up, precision=highest))
    hidden = low(jax.nn.gelu(ffn_inner, approximate=False))
    return residual + jnp.dot(hidden, w_down, precision=highest)

def reference(tokens_in, gain_attn, gain_ffn, w_qkv, w_out, w_up, w_down, slot_mol, slot_fill, cotangent):
    group_size = SLOTS * SLOT_LEN
    mol_all = jnp.repeat(slot_mol, SLOT_LEN, axis=1)
    positions = jnp.arange(group_size, dtype=jnp.int32) % SLOT_LEN
    live_all = positions[None, :] < jnp.repeat(slot_fill, SLOT_LEN, axis=1)

    def forward(input_float, gain_one, gain_two, qkv_float, out_float, up_float, down_float):
        groups = input_float.reshape(GROUPS, group_size, D)

        def per_group(packed):
            group_input, mol_rows, live_rows = packed
            return group_layer(group_input, mol_rows, live_rows, gain_one, gain_two, qkv_float, out_float, up_float, down_float)
        results = lax.map(per_group, (groups, mol_all, live_all))
        return results.reshape(GROUPS * group_size, D)
    output, pullback = jax.vjp(forward, tokens_in.astype(jnp.float32), gain_attn, gain_ffn, w_qkv.astype(jnp.float32), w_out.astype(jnp.float32), w_up.astype(jnp.float32), w_down.astype(jnp.float32))
    grads = pullback(cotangent.astype(jnp.float32))
    return (output.astype(jnp.bfloat16), grads[0], grads[1], grads[2], grads[3], grads[4], grads[5], grads[6])
```

```python
import functools

import jax
import jax.numpy as jnp
from jax import lax
from jax.experimental import pallas as pl
from jax.experimental.pallas import tpu as pltpu
from jax.sharding import PartitionSpec as P

HEAD_DIM = 24
SLOT = 128
D = 768
EPS = 1e-05
SLOTS_DEV = 4
ROWS = SLOTS_DEV * SLOT
WIN = ROWS + 2 * SLOT
BF = jnp.bfloat16
F32 = jnp.float32


def nn(a, b):
    return jnp.dot(a, b, preferred_element_type=F32)


def nt(a, b):
    return lax.dot_general(a, b, (((1,), (1,)), ((), ())), preferred_element_type=F32)


def tn(a, b):
    return lax.dot_general(a, b, (((0,), (0,)), ((), ())), preferred_element_type=F32)


def norm_stats(v):
    mean = jnp.mean(v, axis=-1, keepdims=True)
    centred = v - mean
    var = jnp.mean(centred * centred, axis=-1, keepdims=True)
    r = lax.rsqrt(var + EPS)
    return centred * r, r


def norm_back(grad, z, r, gain):
    e = grad * gain
    return r * (e - jnp.mean(e, -1, keepdims=True) - z * jnp.mean(e * z, -1, keepdims=True))


def build_masks(mask_ref, width):
    rows = lax.broadcasted_iota(jnp.int32, (width, 2 * SLOT), 0)
    right = (lax.broadcasted_iota(jnp.int32, (width, 2 * SLOT), 1) >= SLOT).astype(jnp.int32)
    for p in range(mask_ref.shape[0]):
        low = (2 * p + right) * HEAD_DIM
        keep = (rows >= low) & (rows < low + HEAD_DIM)
        mask_ref[p] = jnp.where(keep, 1.0, 0.0).astype(BF)


def slot_meta(mol_ref, fill_ref, z, s):
    at = z * SLOTS_DEV + s
    last = mol_ref.shape[1] - 1
    before, after = jnp.maximum(at - 1, 0), jnp.minimum(at + 1, last)
    mine = mol_ref[0, at]
    prev = jnp.where((mol_ref[0, before] == mine) & (at > 0), 1, 0)
    nxt = jnp.where((mol_ref[0, after] == mine) & (at < last), 1, 0)
    partner = prev * fill_ref[0, before] + nxt * fill_ref[0, after]
    return prev, nxt, fill_ref[0, at], partner


def key_bias(own, partner):
    at = lax.broadcasted_iota(jnp.int32, (SLOT, SLOT), 0)
    top = jnp.where(at < own, 0.0, -1e30).astype(F32)
    low = jnp.where(at < partner, 0.0, -1e30).astype(F32)
    one = jnp.concatenate([top, low], axis=0)
    return jnp.concatenate([one, one], axis=1)


def pick(flag, a, b):
    keep = jnp.broadcast_to(flag, a.shape) == 1
    return jnp.where(keep, a.astype(F32), b.astype(F32)).astype(a.dtype)


def pair_rows(full):
    rows = lax.broadcasted_iota(jnp.int32, (2 * HEAD_DIM, SLOT), 0)
    return jnp.where(rows < HEAD_DIM, full[:, :SLOT], full[:, SLOT:])


def project(g, parts, nw, qt, kt, vt, kn, vn, scale):
    own = nw[pl.ds(SLOT, ROWS), :]
    qt[g] = (nt(parts[0], own) * scale).astype(BF)
    k = nt(parts[1], nw[...]).astype(BF)
    kt[g] = k
    kn[g] = k.T
    v = nt(parts[2], nw[...]).astype(BF)
    vt[g] = v
    vn[g] = v.T


def windows(s):
    own = pl.multiple_of((s + 1) * SLOT, SLOT)
    before = pl.multiple_of(s * SLOT, SLOT)
    after = pl.multiple_of((s + 2) * SLOT, SLOT)
    return pl.ds(own, SLOT), pl.ds(before, SLOT), pl.ds(after, SLOT), pl.ds(before, SLOT)


def attend(g, s, meta, mask, qt, kn, vt, probs, mixf, mixt):
    prev, _, own_live, partner_live = meta
    own, before, after, mine = windows(s)
    width = qt.shape[1]
    pairs = mask.shape[0]
    keys = jnp.concatenate([kn[g, own, :], pick(prev, kn[g, before, :], kn[g, after, :])], axis=0)
    vals = jnp.concatenate([vt[g, :, own], pick(prev, vt[g, :, before], vt[g, :, after])], axis=1)
    q = qt[g, :, mine]
    q2 = jnp.concatenate([q, q], axis=1)
    bias = key_bias(own_live, partner_live)
    for p in range(pairs):
        scores = nn(keys, q2 * mask[p]) + bias
        top = jnp.max(scores, axis=0, keepdims=True)
        ex = jnp.exp(scores - top)
        total = jnp.sum(ex, axis=0, keepdims=True)
        pr = (ex * (1.0 / total)).astype(BF)
        probs[g, s, p] = pr
        head_rows = slice(2 * HEAD_DIM * p, 2 * HEAD_DIM * (p + 1))
        mixed = pair_rows(nn(vals[head_rows, :], pr))
        mixf[g, head_rows, mine] = mixed
        at = pl.ds(pl.multiple_of(g * width + 2 * HEAD_DIM * p, 16), 2 * HEAD_DIM)
        mixt[at, mine] = mixed.astype(BF)


def attend_back(g, s, meta, mask, qt, kt, vn, dmt, probs, mixf, dqkv, dkt, dvt, scale):
    prev, nxt, _, _ = meta
    own, before, after, mine = windows(s)
    pairs = mask.shape[0]
    fprev, fnext = prev.astype(F32), nxt.astype(F32)
    vals = jnp.concatenate([vn[g, own, :], pick(prev, vn[g, before, :], vn[g, after, :])], axis=0)
    keys = jnp.concatenate([kt[g, :, own], pick(prev, kt[g, :, before], kt[g, :, after])], axis=1)
    q = qt[g, :, mine]
    dm = dmt[g, :, mine]
    q2 = jnp.concatenate([q, q], axis=1)
    dm2 = jnp.concatenate([dm, dm], axis=1)
    prod = dm.astype(F32) * mixf[g, :, mine]
    for p in range(pairs):
        head_rows = slice(2 * HEAD_DIM * p, 2 * HEAD_DIM * (p + 1))
        mid = 2 * HEAD_DIM * p + HEAD_DIM
        inner = jnp.concatenate(
            [
                jnp.sum(prod[2 * HEAD_DIM * p : mid], axis=0, keepdims=True),
                jnp.sum(prod[mid : mid + HEAD_DIM], axis=0, keepdims=True),
            ],
            axis=1,
        )
        rhs = dm2 * mask[p]
        d_probs = nn(vals, rhs)
        pr = probs[g, s, p]
        d_scores = (pr.astype(F32) * (d_probs - inner)).astype(BF)
        dq = pair_rows(nn(keys[head_rows, :], d_scores)) * scale
        dqkv[g, 0, head_rows, mine] = dq.astype(BF)
        qm = (q2 * mask[p])[head_rows, :]
        dk = nt(qm, d_scores)
        dv = nt(rhs[head_rows, :], pr)
        dkt[g, head_rows, own] += dk[:, :SLOT]
        dvt[g, head_rows, own] += dv[:, :SLOT]
        dkt[g, head_rows, before] += fprev * dk[:, SLOT:]
        dvt[g, head_rows, before] += fprev * dv[:, SLOT:]
        dkt[g, head_rows, after] += fnext * dk[:, SLOT:]
        dvt[g, head_rows, after] += fnext * dv[:, SLOT:]


SQH = 0.7071067811865476
PHI = 0.3989422804014327
MESH = pl.DeviceIdType.MESH
HALVINGS = 3
PIECE = D // 8
LANE = PIECE // 2


class Link:
    def __init__(self, send_sem, recv_sem):
        self.send_sem, self.recv_sem, self.used, self.open = send_sem, recv_sem, 0, []

    def make(self, src, dst, target):
        slot = self.used
        self.used += 1
        return pltpu.make_async_remote_copy(
            src_ref=src, dst_ref=dst, send_sem=self.send_sem.at[slot], recv_sem=self.recv_sem.at[slot],
            device_id=target, device_id_type=MESH,
        )

    def send(self, src, dst, target):
        copy = self.make(src, dst, target)
        copy.start()
        self.open.append(copy)
        return copy

    def done(self, copy):
        copy.wait_send()
        self.open = [c for c in self.open if c is not copy]

    def drain(self):
        for copy in self.open:
            copy.wait_send()
        self.open = []


def add_rows(dst, *terms):
    if len(dst.shape) == 3:
        for unit in range(dst.shape[0]):
            add_rows(dst.at[unit], *[term.at[unit] for term in terms])
        return

    @pl.loop(0, dst.shape[0] // 16)
    def _(i):
        at = pl.ds(pl.multiple_of(i * 16, 16), 16)
        total = dst[at, :].astype(F32)
        for term in terms:
            total = total + term[at, :].astype(F32)
        dst[at, :] = total.astype(dst.dtype)


def piece_rows(d0, d1, d2, lane):
    return pl.ds(pl.multiple_of(((d0 * 2 + d1) * 2 + d2) * PIECE + lane * LANE, 16), LANE)


def half_rows(d0):
    return pl.ds(pl.multiple_of(d0 * (D // 2), 16), D // 2)


def take(ref, rows):
    return ref.at[:, rows] if len(ref.shape) == 3 else ref.at[rows]


class Place:
    def __init__(self, dp_size, shards):
        self.dp = lax.axis_index("dp")
        self.z = lax.axis_index("head")
        self.shards = shards
        self.bits, self.partner = [], []
        step = 1
        while step < dp_size:
            bit = (self.dp // step) % 2
            self.bits.append(bit)
            self.partner.append(self.dp + step - 2 * step * bit)
            step *= 2
        self.order = ((0, 1, 2), (0, 2, 1))

    def near(self, bit):
        return {"dp": self.partner[bit]}

    def across(self, k):
        step, found = 1, 0
        while step < self.shards:
            bit = (self.z // step) % 2
            found = found + step * ((bit + 1) % 2 if (k // step) % 2 else bit)
            step *= 2
        return found

    def index(self, lane):
        return tuple(self.bits[b] for b in self.order[lane])


class Halve:
    def __init__(self, link, place, g, r0, r1, r2, rx):
        self.link, self.place, self.g, self.r0, self.r1, self.r2, self.rx = link, place, g, r0, r1, r2, rx

    def start(self):
        c0 = self.place.bits[0]
        self.copies = [self.link.send(take(self.g, half_rows(1 - c0)), self.r0, self.place.near(0))]

    def mine(self, lane):
        return take(self.g, piece_rows(*self.place.index(lane), lane))

    def step1(self):
        p = self.place
        self.copies[0].wait_recv()
        self.copies = []
        for lane in range(2):
            c0, c1, _ = p.index(lane)
            sent = []
            for b in range(2):
                part = take(self.g, piece_rows(c0, 1 - c1, b, lane))
                add_rows(part, take(self.r0, piece_rows(0, 1 - c1, b, lane)))
                sent.append(self.link.send(part, self.r1.at[lane, b], p.near(p.order[lane][1])))
            self.copies.append(sent)
        for lane in range(2):
            c0, c1, _ = p.index(lane)
            for b in range(2):
                add_rows(take(self.g, piece_rows(c0, c1, b, lane)), take(self.r0, piece_rows(0, c1, b, lane)))

    def step2(self):
        p = self.place
        old, self.copies = self.copies, []
        for lane in range(2):
            c0, c1, c2 = p.index(lane)
            for copy in old[lane]:
                copy.wait_recv()
            part = take(self.g, piece_rows(c0, c1, 1 - c2, lane))
            add_rows(part, self.r1.at[lane, 1 - c2])
            self.copies.append(self.link.send(part, self.r2.at[lane], p.near(p.order[lane][2])))
        for lane in range(2):
            _, _, c2 = p.index(lane)
            add_rows(self.mine(lane), self.r1.at[lane, c2])

    def step3(self):
        p = self.place
        for lane in range(2):
            self.copies[lane].wait_recv()
            add_rows(self.mine(lane), self.r2.at[lane])
        for extra in range(HALVINGS, len(p.bits)):
            copies = [
                self.link.send(self.mine(lane), self.rx.at[extra - HALVINGS, lane], p.near(extra)) for lane in range(2)
            ]
            for lane in range(2):
                copies[lane].wait_recv()
                self.link.done(copies[lane])
                add_rows(self.mine(lane), self.rx.at[extra - HALVINGS, lane])


class Spread:
    def __init__(self, link, place, f):
        self.link, self.place, self.f = link, place, f

    def swap(self, rows, bit):
        part = take(self.f, rows)
        return self.link.send(part, part, self.place.near(bit))

    def start(self):
        p = self.place
        self.copies = [[self.swap(piece_rows(*p.index(lane), lane), p.order[lane][2])] for lane in range(2)]

    def step1(self):
        p = self.place
        old, self.copies = self.copies, []
        for lane in range(2):
            c0, c1, _ = p.index(lane)
            for copy in old[lane]:
                copy.wait_recv()
            self.copies.append([self.swap(piece_rows(c0, c1, b, lane), p.order[lane][1]) for b in range(2)])

    def step2(self):
        for lane in range(2):
            for copy in self.copies[lane]:
                copy.wait_recv()
        self.copies = [self.swap(half_rows(self.place.bits[0]), 0)]

    def finish(self):
        self.copies[0].wait_recv()


def kernel(
    dp_size, shards,
    mol, fill, x, cot, gain_a, gain_f, wown, wu, wd,
    out, dtok, gains_out, f_ud, f_own,
    wg, nw, xh, mask, qt, kt, vt, kn, vn, probs, mixf, mixt, dmt, dbr, dres,
    dqkv, dkt, dvt, halo_out, halo_in, g_ud, g_k, r0u, r1u, r2u, rxu, r0, r1, r2, rx, zud, zk,
    gain_sum, gain_got, gain_col,
    send_sem, recv_sem, halo_send, halo_recv, load_sem,
):
    place = Place(dp_size, shards)
    link = Link(send_sem, recv_sem)
    z = place.z
    last = shards - 1
    nffn, hidden, dinner = (g_k.at[i, pl.ds(0, ROWS)] for i in range(3))
    scale = HEAD_DIM ** (-0.5)
    width = qt.shape[1]

    def column(k):
        return {"head": place.across(k)}

    barrier = pltpu.get_barrier_semaphore()
    peers = [place.near(b) for b in range(len(place.bits))] + [column(k) for k in range(1, shards)]
    for peer in peers:
        pl.semaphore_signal(barrier, inc=1, device_id=peer, device_id_type=MESH)
    pl.semaphore_wait(barrier, len(peers))

    own_w = pltpu.make_async_copy(wown, wg.at[z], load_sem)
    own_w.start()
    after = {"head": jnp.minimum(z + 1, last)}
    before = {"head": jnp.maximum(z - 1, 0)}
    to_next = link.make(x.at[pl.ds(ROWS - SLOT, SLOT)], xh.at[0], after)
    to_prev = link.make(x.at[pl.ds(0, SLOT)], xh.at[1], before)

    @pl.when(z < last)
    def _():
        to_next.start()

    @pl.when(z > 0)
    def _():
        to_prev.start()

    gather = []
    for k in range(1, shards):
        copies = []
        for lane in range(2):
            rows = piece_rows(*place.index(lane), lane)
            copies.append(link.send(wown.at[rows], wg.at[z, rows], column(k)))
        gather.append((copies, Spread(link, place, wg.at[place.across(k)])))

    build_masks(mask, width)

    def normed(at_w, ref, at):
        zz, _ = norm_stats(ref[at, :].astype(F32))
        nw[at_w, :] = (zz * gain_a[...]).astype(BF)

    @pl.loop(0, ROWS // 64)
    def _(i):
        at = pl.multiple_of(i * 64, 64)
        normed(pl.ds(at + SLOT, 64), x, pl.ds(at, 64))

    @pl.when(z > 0)
    def _():
        to_next.wait_recv()

    @pl.when(z == 0)
    def _():
        xh[0] = jnp.zeros_like(xh[0])

    @pl.when(z < last)
    def _():
        to_prev.wait_recv()

    @pl.when(z == last)
    def _():
        xh[1] = jnp.zeros_like(xh[1])

    @pl.loop(0, SLOT // 64)
    def _(i):
        at = pl.multiple_of(i * 64, 64)
        normed(pl.ds(at, 64), xh.at[0], pl.ds(at, 64))
        normed(pl.ds(at + SLOT + ROWS, 64), xh.at[1], pl.ds(at, 64))

    def weight(g, c):
        return wg[g, c * width : (c + 1) * width, :]

    def forward(g):
        project(g, [weight(g, c) for c in range(3)], nw, qt, kt, vt, kn, vn, scale)

        @pl.loop(0, SLOTS_DEV)
        def _(s):
            attend(g, s, slot_meta(mol, fill, z, s), mask, qt, kn, vt, probs, mixf, mixt)

    own_w.wait()
    forward(z)
    for copies, spread in gather:
        for copy in copies:
            copy.wait_recv()
        spread.start()
    for _, spread in gather:
        spread.step1()
    for _, spread in gather:
        spread.step2()
    for k in range(1, shards):
        gather[k - 1][1].finish()
        forward(place.across(k))

    mixn = mixt[...].T
    total = x[...].astype(F32)
    for g in range(shards):
        total = total + nn(mixn[:, g * width : (g + 1) * width], weight(g, 3))
    dres[...] = total

    gain_sum[...] = jnp.zeros_like(gain_sum)

    @pl.loop(0, ROWS // 64)
    def _(i):
        at = pl.ds(pl.multiple_of(i * 64, 64), 64)
        zz, _ = norm_stats(dres[at, :])
        nffn[at, :] = (zz * gain_f[...]).astype(BF)

    BLK = 256

    @pl.loop(0, ROWS // BLK)
    def _(i):
        at = pl.ds(pl.multiple_of(i * BLK, BLK), BLK)
        u = nn(nffn[at, :], wu[...])
        c = cot[at, :]
        dh = nt(c, wd[...])
        cdf = 0.5 + 0.5 * lax.erf(u * SQH)
        h = (u * cdf).astype(BF)
        hidden[at, :] = h
        dinner[at, :] = (dh * (cdf + u * (PHI * jnp.exp(-0.5 * u * u)))).astype(BF)
        out[at, :] = (dres[at, :] + nn(h, wd[...])).astype(BF)

    g_ud[1] = tn(hidden[...], cot[...]).astype(BF)
    g_ud[0] = tn(nffn[...], dinner[...]).astype(BF)
    ud = Halve(link, place, g_ud, r0u, r1u, r2u, rxu)
    ud.start()

    @pl.loop(0, ROWS // BLK)
    def _(i):
        at = pl.ds(pl.multiple_of(i * BLK, BLK), BLK)
        dn = nt(dinner[at, :], wu[...])
        zz, r = norm_stats(dres[at, :])
        gain_sum[1:2, :] += jnp.sum(dn * zz, axis=0, keepdims=True)
        dr = cot[at, :].astype(F32) + norm_back(dn, zz, r, gain_f[...])
        dres[at, :] = dr
        dbr[at, :] = dr.astype(BF)

    dkt[...] = jnp.zeros_like(dkt)
    dvt[...] = jnp.zeros_like(dvt)

    def back(g, s):
        attend_back(
            g, s, slot_meta(mol, fill, z, s), mask, qt, kt, vn, dmt, probs, mixf, dqkv, dkt, dvt, scale
        )

    def halo_copy(side, g):
        return pltpu.make_async_remote_copy(
            src_ref=halo_out.at[side, g], dst_ref=halo_in.at[side, g],
            send_sem=halo_send.at[side, g], recv_sem=halo_recv.at[side, g],
            device_id=after if side else before, device_id_type=MESH,
        )

    def border(g):
        dmt[g] = nt(wg[g, 3 * width : 4 * width, :], dbr[...]).astype(BF)
        back(g, 0)
        back(g, SLOTS_DEV - 1)
        for side, cols in ((0, slice(0, SLOT)), (1, slice(SLOT + ROWS, WIN))):
            halo_out[side, g, 0] = dkt[g, :, cols].astype(BF)
            halo_out[side, g, 1] = dvt[g, :, cols].astype(BF)

        @pl.when(z > 0)
        def _():
            halo_copy(0, g).start()

        @pl.when(z < last)
        def _():
            halo_copy(1, g).start()

    ud_steps = [ud.step1, ud.step2, ud.step3]
    for k in range(shards):
        border(place.across((k + 1) % shards))
        if k < 3:
            ud_steps[k]()

    def quarter(ref, q):
        lane = q % 2
        c0, ca, cb = place.index(0)
        rows = piece_rows(c0, ca + lane * (cb - ca), cb + lane * (ca - cb), lane)
        return ref.at[q // 2, rows]

    z_copies = [
        link.send(quarter(g_ud, place.across(k)), zud.at[k - 1], column(k)) for k in range(1, shards)
    ]
    spread_ud = Spread(link, place, f_ud)
    own_spread = Spread(link, place, f_own)

    def ud_sum():
        for copy in z_copies:
            copy.wait_recv()
        mine = quarter(g_ud, z)
        add_rows(mine, *[zud.at[k] for k in range(shards - 1)])
        quarter(f_ud, z)[...] = mine[...]
        return [link.send(quarter(f_ud, z), quarter(f_ud, z), column(k)) for k in range(1, shards)]

    def ud_spread():
        for copy in z_back:
            copy.wait_recv()
        spread_ud.start()

    def shard_grads(k):
        g = place.across(k)

        @pl.loop(1, SLOTS_DEV - 1)
        def _(s):
            back(g, s)

        @pl.when(z < last)
        def _():
            halo_copy(0, g).wait_recv()
            cols = slice(ROWS, SLOT + ROWS)
            dkt[g, :, cols] += halo_in[0, g, 0].astype(F32)
            dvt[g, :, cols] += halo_in[0, g, 1].astype(F32)

        @pl.when(z > 0)
        def _():
            halo_copy(1, g).wait_recv()
            cols = slice(SLOT, 2 * SLOT)
            dkt[g, :, cols] += halo_in[1, g, 0].astype(F32)
            dvt[g, :, cols] += halo_in[1, g, 1].astype(F32)

        dqkv[g, 1] = dkt[g, :, SLOT : SLOT + ROWS].astype(BF)
        dqkv[g, 2] = dvt[g, :, SLOT : SLOT + ROWS].astype(BF)
        own = nw[SLOT : SLOT + ROWS, :]
        for c in range(3):
            g_k[k, c * width : (c + 1) * width, :] = nn(dqkv[g, c], own).astype(BF)
        at = pl.ds(pl.multiple_of(g * width, 16), width)
        g_k[k, 3 * width : 4 * width, :] = nn(mixt[at, :], dbr[...]).astype(BF)
        job = Halve(link, place, g_k.at[k], r0.at[k], r1.at[k], r2.at[k], rx.at[k])
        job.start()
        return job

    def send_shard(k, job):
        return [link.send(job.mine(lane), zk.at[k - 1, lane], column(k)) for lane in range(2)]

    job1 = shard_grads(1)
    z_back = ud_sum()
    job2 = shard_grads(2)
    job1.step1()
    ud_spread()
    job3 = shard_grads(3)
    job1.step2()
    job2.step1()
    spread_ud.step1()
    job0 = shard_grads(0)
    job1.step3()
    z1 = send_shard(1, job1)
    job2.step2()
    job3.step1()
    spread_ud.step2()

    total = None
    for g in range(shards):
        term = tn(dqkv[g].reshape(3 * width, ROWS), wg[g, : 3 * width, :])
        total = term if total is None else total + term
    dtok[...] = total
    job0.step1()
    job2.step3()
    z2 = send_shard(2, job2)
    job3.step2()

    @pl.loop(0, ROWS // 64)
    def _(i):
        at = pl.ds(pl.multiple_of(i * 64, 64), 64)
        dn = dtok[at, :]
        zz, r = norm_stats(x[at, :].astype(F32))
        gain_sum[0:1, :] += jnp.sum(dn * zz, axis=0, keepdims=True)
        dtok[at, :] = dres[at, :] + norm_back(dn, zz, r, gain_a[...])

    job0.step2()
    job3.step3()
    z3 = send_shard(3, job3)
    spread_ud.finish()

    for bit in range(len(place.bits)):
        copy = link.send(gain_sum, gain_got.at[bit], place.near(bit))
        copy.wait_recv()
        link.done(copy)
        gain_sum[...] += gain_got[bit]
    gain_col[z] = gain_sum[...]
    gain_copies = [link.send(gain_sum, gain_col.at[z], column(k)) for k in range(1, shards)]

    job0.step3()
    for copy in z1 + z2 + z3:
        copy.wait_recv()
    for lane in range(2):
        mine = job0.mine(lane)
        add_rows(mine, *[zk.at[k, lane] for k in range(shards - 1)])
        f_own.at[piece_rows(*place.index(lane), lane)][...] = mine[...]
    own_spread.start()
    own_spread.step1()
    own_spread.step2()
    for copy in gain_copies:
        copy.wait_recv()
    gains_out[...] = sum(gain_col[k] for k in range(shards))
    own_spread.finish()

    link.drain()

    @pl.when(z < last)
    def _():
        to_next.wait_send()
        for g in range(shards):
            halo_copy(1, g).wait_send()

    @pl.when(z > 0)
    def _():
        to_prev.wait_send()
        for g in range(shards):
            halo_copy(0, g).wait_send()


VM = pl.BlockSpec(memory_space=pltpu.VMEM)
SM = pl.BlockSpec(memory_space=pltpu.SMEM)
COPIES = 96


def S(shape, dtype):
    return jax.ShapeDtypeStruct(shape, dtype)


def layer(dp_size, n, width, *operands):
    pairs = width // (2 * HEAD_DIM)
    extra = 1
    step = 8
    more = 0
    while step < dp_size:
        step *= 2
        more += 1
    extra = max(more, 1)
    bits = 3 + more
    V = pltpu.VMEM
    return pl.pallas_call(
        functools.partial(kernel, dp_size, n),
        out_shape=(S((ROWS, D), BF), S((ROWS, D), F32), S((8, D), F32), S((2, D, D), BF), S((D, D), BF)),
        in_specs=[SM, SM] + [VM] * 4 + [pl.BlockSpec(memory_space=pl.ANY)] + [VM] * 2,
        out_specs=(VM,) * 5,
        scratch_shapes=[
            V((n, D, D), BF),
            V((WIN, D), BF),
            V((2, SLOT, D), BF),
            V((pairs, width, 2 * SLOT), BF),
            V((n, width, ROWS), BF),
            V((n, width, WIN), BF),
            V((n, width, WIN), BF),
            V((n, WIN, width), BF),
            V((n, WIN, width), BF),
            V((n, SLOTS_DEV, pairs, 2 * SLOT, 2 * SLOT), BF),
            V((n, width, ROWS), F32),
            V((D, ROWS), BF),
            V((n, width, ROWS), BF),
            V((ROWS, D), BF),
            V((ROWS, D), F32),
            V((n, 3, width, ROWS), BF),
            V((n, width, WIN), F32),
            V((n, width, WIN), F32),
            V((2, n, 2, width, SLOT), BF),
            V((2, n, 2, width, SLOT), BF),
            V((2, D, D), BF),
            V((n, D, D), BF),
            V((2, D // 2, D), BF),
            V((2, 2, 2, LANE, D), BF),
            V((2, 2, LANE, D), BF),
            V((extra, 2, 2, LANE, D), BF),
            V((n, D // 2, D), BF),
            V((n, 2, 2, LANE, D), BF),
            V((n, 2, LANE, D), BF),
            V((n, extra, 2, LANE, D), BF),
            V((n - 1, LANE, D), BF),
            V((n - 1, 2, LANE, D), BF),
            V((8, D), F32),
            V((bits, 8, D), F32),
            V((n, 8, D), F32),
            pltpu.SemaphoreType.DMA((COPIES + 12 * more,)),
            pltpu.SemaphoreType.DMA((COPIES + 12 * more,)),
            pltpu.SemaphoreType.DMA((2, n)),
            pltpu.SemaphoreType.DMA((2, n)),
            pltpu.SemaphoreType.DMA,
        ],
        compiler_params=pltpu.CompilerParams(
            vmem_limit_bytes=67043328, collective_id=0, has_side_effects=True
        ),
        name="layer",
    )(*operands)


def local(tokens_in, gain_attn, gain_ffn, w_qkv, w_out, w_up, w_down, slot_mol, slot_fill, cotangent):
    n = lax.axis_size("head")
    width = w_out.shape[0]
    wown = jnp.concatenate([w_qkv.transpose(0, 2, 1).reshape(3 * width, D), w_out], axis=0)
    out, dtok, gains, ud, own = layer(
        lax.axis_size("dp"), n, width,
        slot_mol, slot_fill, tokens_in, cotangent, gain_attn[None], gain_ffn[None], wown, w_up, w_down,
    )
    own = own.astype(F32)
    ud = ud.astype(F32)
    gqkv = own[: 3 * width].reshape(3, width, D).transpose(0, 2, 1)
    return (out, dtok, gains[0], gains[1], gqkv, own[3 * width :], ud[0], ud[1])


def solution(mesh):
    return jax.shard_map(
        local,
        mesh=mesh,
        in_specs=(
            P(("dp", "head"), None), P(), P(), P(None, None, "head"), P("head", None), P(), P(),
            P("dp", None), P("dp", None), P(("dp", "head"), None),
        ),
        out_specs=(
            P(("dp", "head"), None), P(("dp", "head"), None), P(), P(), P(None, None, "head"), P("head", None), P(), P(),
        ),
        check_vma=False,
    )
```

```python
import functools

import jax
import jax.numpy as jnp
from jax import lax
from jax.experimental import pallas as pl
from jax.experimental.pallas import tpu as pltpu
from jax.sharding import PartitionSpec as P

HEAD_DIM = 24
SLOT = 128
D = 768
EPS = 1e-05
SLOTS_DEV = 4
ROWS = SLOTS_DEV * SLOT
WIN = ROWS + 2 * SLOT
BF = jnp.bfloat16
F32 = jnp.float32


def nn(a, b):
    return jnp.dot(a, b, preferred_element_type=F32)


def nt(a, b):
    return lax.dot_general(a, b, (((1,), (1,)), ((), ())), preferred_element_type=F32)


def tn(a, b):
    return lax.dot_general(a, b, (((0,), (0,)), ((), ())), preferred_element_type=F32)


def norm_stats(v):
    mean = jnp.mean(v, axis=-1, keepdims=True)
    centred = v - mean
    var = jnp.mean(centred * centred, axis=-1, keepdims=True)
    r = lax.rsqrt(var + EPS)
    return centred * r, r


def norm_back(grad, z, r, gain):
    e = grad * gain
    return r * (e - jnp.mean(e, -1, keepdims=True) - z * jnp.mean(e * z, -1, keepdims=True))


WIDER = 64


def build_masks(mask_ref, width):
    shape = mask_ref.shape[1:]
    rows = lax.broadcasted_iota(jnp.int32, shape, 0)
    right = (lax.broadcasted_iota(jnp.int32, shape, 1) >= SLOT).astype(jnp.int32)
    for p in range(mask_ref.shape[0]):
        low = (2 * p + right) * HEAD_DIM
        keep = ((rows >= low) & (rows < low + HEAD_DIM)) | (rows >= width)
        mask_ref[p] = jnp.where(keep, 1.0, 0.0).astype(BF)


def extend(fill_ref, z, width, qt, kt, vt, kn, vn):
    lane = lax.broadcasted_iota(jnp.int32, (SLOT, WIDER), 1)
    row = lax.broadcasted_iota(jnp.int32, (SLOT, WIDER), 0)
    ones = jnp.where(lane < 2, 1.0, 0.0).astype(BF)
    top = lax.broadcasted_iota(jnp.int32, (WIDER, ROWS), 0)
    first = jnp.where(top == 0, 1.0, 0.0).astype(BF)
    slots = (WIN + SLOT) // SLOT
    for g in range(qt.shape[0]):
        qt[g, width:, :] = first
        kn[g, WIN:, :width] = jnp.zeros((SLOT, width), BF)
    for s in range(slots):
        live = 0
        if s < slots - 1:
            at = jnp.minimum(jnp.maximum(z * SLOTS_DEV + s - 1, 0), fill_ref.shape[1] - 1)
            live = fill_ref[0, at]
        bias = jnp.where((lane == 0) & (row >= live), -1e30, 0.0).astype(BF)
        for g in range(qt.shape[0]):
            kn[g, s * SLOT : (s + 1) * SLOT, width:] = bias
            if s < slots - 1:
                vn[g, s * SLOT : (s + 1) * SLOT, width:] = ones


def slot_meta(mol_ref, z, s):
    at = z * SLOTS_DEV + s
    last = mol_ref.shape[1] - 1
    before, after = jnp.maximum(at - 1, 0), jnp.minimum(at + 1, last)
    mine = mol_ref[0, at]
    prev = jnp.where((mol_ref[0, before] == mine) & (at > 0), 1, 0)
    nxt = jnp.where((mol_ref[0, after] == mine) & (at < last), 1, 0)
    return prev, nxt * (1 - prev)


def chosen(*terms):
    total = None
    for flag, block in terms:
        term = jnp.broadcast_to(flag.astype(F32), block.shape).astype(BF) * block
        total = term if total is None else total + term
    return total


def pair_rows(full):
    rows = lax.broadcasted_iota(jnp.int32, (2 * HEAD_DIM, SLOT), 0)
    return jnp.where(rows < HEAD_DIM, full[:, :SLOT], full[:, SLOT:])


def project(g, parts, nw, low, count, qt, kt, vt, kn, vn, scale):
    width = kt.shape[1]
    at = slice(low, low + count)
    if parts[0] is not None:
        qt[g, :width, :] = (nt(parts[0], nw[pl.ds(SLOT, ROWS), :]) * scale).astype(BF)
    for part, wide, tall in ((parts[1], kt, kn), (parts[2], vt, vn)):
        rows = nt(part, nw[at, :]).astype(BF)
        wide[g, :, at] = rows
        tall[g, at, :width] = rows.T


def windows(s):
    own = pl.multiple_of((s + 1) * SLOT, SLOT)
    before = pl.multiple_of(s * SLOT, SLOT)
    after = pl.multiple_of((s + 2) * SLOT, SLOT)
    return pl.ds(own, SLOT), pl.ds(before, SLOT), pl.ds(after, SLOT), pl.ds(before, SLOT)


def attend(g, s, meta, mask, qt, kn, vt, probs, share, mixf, mixt):
    prev, nxt = meta
    own, before, after, mine = windows(s)
    width = vt.shape[1]
    partner = chosen((prev, kn[g, before, :]), (nxt, kn[g, after, :]), (1 - prev - nxt, kn[g, WIN:, :]))
    keys = jnp.concatenate([kn[g, own, :], partner], axis=0)
    vals = jnp.concatenate([vt[g, :, own], chosen((prev, vt[g, :, before]), (nxt, vt[g, :, after]))], axis=1)
    ones = jnp.ones((16, 2 * SLOT), BF)
    q = qt[g, :, mine]
    q2 = jnp.concatenate([q, q], axis=1)
    for p in range(mask.shape[0]):
        scores = nn(keys, q2 * mask[p])
        top = jnp.max(scores, axis=0, keepdims=True)
        ex = jnp.exp(scores - top).astype(BF)
        probs[g, s, p] = ex
        head_rows = slice(2 * HEAD_DIM * p, 2 * HEAD_DIM * (p + 1))
        both = nn(jnp.concatenate([vals[head_rows, :], ones], axis=0), ex)
        part = pair_rows(jnp.broadcast_to(1.0 / both[2 * HEAD_DIM : 2 * HEAD_DIM + 1, :], (2 * HEAD_DIM, 2 * SLOT)))
        mixed = pair_rows(both[: 2 * HEAD_DIM, :]) * part
        share[g, head_rows, mine] = part
        mixf[g, head_rows, mine] = mixed
        at = pl.ds(pl.multiple_of(g * width + 2 * HEAD_DIM * p, 16), 2 * HEAD_DIM)
        mixt[at, mine] = mixed.astype(BF)


def attend_back(g, s, meta, mask, qt, kt, vn, dmt, probs, share, mixf, dqkv, dkt, dvt, scale):
    prev, nxt = meta
    own, before, after, mine = windows(s)
    width = dmt.shape[1]
    fprev, fnext = prev.astype(F32), nxt.astype(F32)
    vals = jnp.concatenate([vn[g, own, :], chosen((prev, vn[g, before, :]), (nxt, vn[g, after, :]))], axis=0)
    keys = jnp.concatenate([kt[g, :, own], chosen((prev, kt[g, :, before]), (nxt, kt[g, :, after]))], axis=1)
    q = qt[g, :width, mine]
    dm = (dmt[g, :, mine].astype(F32) * share[g, :, mine]).astype(BF)
    q2 = jnp.concatenate([q, q], axis=1)
    dm2 = jnp.concatenate([dm, dm], axis=1)
    prod = dm.astype(F32) * mixf[g, :, mine]
    line = lax.broadcasted_iota(jnp.int32, (16, 2 * SLOT), 0)
    rest = jnp.zeros((WIDER - 16, 2 * SLOT), BF)
    for p in range(mask.shape[0]):
        head_rows = slice(2 * HEAD_DIM * p, 2 * HEAD_DIM * (p + 1))
        mid = 2 * HEAD_DIM * p + HEAD_DIM
        inner = jnp.concatenate(
            [
                jnp.sum(prod[2 * HEAD_DIM * p : mid], axis=0, keepdims=True),
                jnp.sum(prod[mid : mid + HEAD_DIM], axis=0, keepdims=True),
            ],
            axis=1,
        )
        high = inner.astype(BF).astype(F32)
        take_off = jnp.where(line == 0, -high, jnp.where(line == 1, high - inner, 0.0)).astype(BF)
        rhs = dm2 * mask[p, :width, :]
        d_probs = nn(vals, jnp.concatenate([rhs, take_off, rest], axis=0))
        pr = probs[g, s, p]
        d_scores = pr * d_probs.astype(BF)
        dq = pair_rows(nn(keys[head_rows, :], d_scores)) * scale
        dqkv[g, 0, head_rows, mine] = dq.astype(BF)
        qm = (q2 * mask[p, :width, :])[head_rows, :]
        dk = nt(qm, d_scores)
        dv = nt(rhs[head_rows, :], pr)
        dkt[g, head_rows, own] += dk[:, :SLOT]
        dvt[g, head_rows, own] += dv[:, :SLOT]
        dkt[g, head_rows, before] += fprev * dk[:, SLOT:]
        dvt[g, head_rows, before] += fprev * dv[:, SLOT:]
        dkt[g, head_rows, after] += fnext * dk[:, SLOT:]
        dvt[g, head_rows, after] += fnext * dv[:, SLOT:]


SQH = 0.7071067811865476
PHI = 0.3989422804014327
MESH = pl.DeviceIdType.MESH
HALVINGS = 3
PIECE = D // 8
LANE = PIECE // 2


class Link:
    def __init__(self, send_sem, recv_sem):
        self.send_sem, self.recv_sem, self.used, self.open = send_sem, recv_sem, 0, []

    def reserve(self, count):
        self.used += count
        return self.used - count

    def make(self, src, dst, target, slot=None):
        slot = self.reserve(1) if slot is None else slot
        return pltpu.make_async_remote_copy(
            src_ref=src, dst_ref=dst, send_sem=self.send_sem.at[slot], recv_sem=self.recv_sem.at[slot],
            device_id=target, device_id_type=MESH,
        )

    def send(self, src, dst, target):
        copy = self.make(src, dst, target)
        copy.start()
        self.open.append(copy)
        return copy

    def done(self, copy):
        copy.wait_send()
        self.open = [c for c in self.open if c is not copy]

    def drain(self):
        for copy in self.open:
            copy.wait_send()
        self.open = []


def add_rows(dst, *terms):
    @pl.loop(0, dst.shape[0] // 16)
    def _(i):
        at = pl.ds(pl.multiple_of(i * 16, 16), 16)
        total = dst[at, :].astype(F32)
        for term in terms:
            total = total + term[at, :].astype(F32)
        dst[at, :] = total.astype(dst.dtype)


def piece_rows(d0, d1, d2, lane):
    return pl.ds(pl.multiple_of(((d0 * 2 + d1) * 2 + d2) * PIECE + lane * LANE, 16), LANE)


class Place:
    def __init__(self, dp_size, shards):
        self.dp = lax.axis_index("dp")
        self.z = lax.axis_index("head")
        self.shards = shards
        self.bits, self.partner = [], []
        step = 1
        while step < dp_size:
            bit = (self.dp // step) % 2
            self.bits.append(bit)
            self.partner.append(self.dp + step - 2 * step * bit)
            step *= 2
        self.order = ((0, 1, 2), (0, 2, 1))

    def near(self, bit):
        return {"dp": self.partner[bit]}

    def across(self, k):
        step, found = 1, 0
        while step < self.shards:
            found = found + step * ((self.z // step + k // step) % 2)
            step *= 2
        return found

    def index(self, lane):
        return tuple(self.bits[b] for b in self.order[lane])


class Halve:
    def __init__(self, link, place, g, r0, r1, r2, rx):
        self.link, self.place, self.g, self.r0, self.r1, self.r2, self.rx = link, place, g, r0, r1, r2, rx

    def start(self):
        p = self.place
        self.pass_on, self.keep = [], []
        for side, out in ((1, self.pass_on), (0, self.keep)):
            for lane in range(2):
                c0, c1, _ = p.index(lane)
                d1 = c1 + side * (1 - 2 * c1)
                out.append(
                    [
                        self.link.send(
                            self.g.at[piece_rows(1 - c0, d1, b, lane)], self.r0.at[piece_rows(0, d1, b, lane)], p.near(0)
                        )
                        for b in range(2)
                    ]
                )

    def mine(self, lane):
        return self.g.at[piece_rows(*self.place.index(lane), lane)]

    def step1(self):
        p = self.place
        self.copies = []
        for lane in range(2):
            c0, c1, _ = p.index(lane)
            sent = []
            for b in range(2):
                self.pass_on[lane][b].wait_recv()
                part = self.g.at[piece_rows(c0, 1 - c1, b, lane)]
                add_rows(part, self.r0.at[piece_rows(0, 1 - c1, b, lane)])
                sent.append(self.link.send(part, self.r1.at[lane, b], p.near(p.order[lane][1])))
            self.copies.append(sent)

    def step2(self, finish=None, r_last=None):
        p = self.place
        old, self.copies = self.copies, []
        for lane in range(2):
            c0, c1, c2 = p.index(lane)
            for b in range(2):
                self.keep[lane][b].wait_recv()
                old[lane][b].wait_recv()
            if finish is not None:
                for b in range(2):
                    part = self.g.at[piece_rows(c0, c1, b, lane)]
                    add_rows(part, self.r0.at[piece_rows(0, c1, b, lane)], self.r1.at[lane, b])
                finish(lane)
                self.copies.append(
                    [
                        self.link.send(self.g.at[piece_rows(c0, c1, b, lane)], r_last.at[lane, b], p.near(p.order[lane][2]))
                        for b in range(2)
                    ]
                )
                continue
            part = self.g.at[piece_rows(c0, c1, 1 - c2, lane)]
            add_rows(part, self.r0.at[piece_rows(0, c1, 1 - c2, lane)], self.r1.at[lane, 1 - c2])
            self.copies.append(self.link.send(part, self.r2.at[lane], p.near(p.order[lane][2])))

    def step3(self):
        p = self.place
        for lane in range(2):
            _, c1, c2 = p.index(lane)
            self.copies[lane].wait_recv()
            add_rows(self.mine(lane), self.r0.at[piece_rows(0, c1, c2, lane)], self.r1.at[lane, c2], self.r2.at[lane])
        for extra in range(HALVINGS, len(p.bits)):
            copies = [
                self.link.send(self.mine(lane), self.rx.at[extra - HALVINGS, lane], p.near(extra)) for lane in range(2)
            ]
            for lane in range(2):
                copies[lane].wait_recv()
                self.link.done(copies[lane])
                add_rows(self.mine(lane), self.rx.at[extra - HALVINGS, lane])


    def step3_both(self, r_last, spread):
        p = self.place
        spread.begin()
        for lane in range(2):
            c0, c1, c2 = p.index(lane)
            for b in range(2):
                self.copies[lane][b].wait_recv()
            for b in range(2):
                rows = piece_rows(c0, c1, b, lane)
                self.link.done(self.copies[lane][b])
                add_rows(self.g.at[rows], r_last.at[lane, b])
                spread.f.at[rows][...] = self.g.at[rows][...]
            for b in range(2):
                spread.pass_on(lane, piece_rows(c0, c1, b, lane))


class Spread:
    def __init__(self, link, place, f):
        self.link, self.place, self.f = link, place, f

    def swap(self, rows, bit):
        part = self.f.at[rows]
        return self.link.send(part, part, self.place.near(bit))

    def begin(self):
        self.first, self.second, self.core = [], [[], []], []

    def pass_on(self, lane, rows):
        self.second[lane].append(self.swap(rows, self.place.order[lane][1]))
        self.core.append(self.swap(rows, 0))

    def start(self):
        p = self.place
        self.begin()
        for lane in range(2):
            own = piece_rows(*p.index(lane), lane)
            self.first.append(self.swap(own, p.order[lane][2]))
            self.pass_on(lane, own)

    def step1(self):
        p = self.place
        for lane in range(2):
            c0, c1, c2 = p.index(lane)
            self.first[lane].wait_recv()
            self.pass_on(lane, piece_rows(c0, c1, 1 - c2, lane))

    def step2(self):
        p = self.place
        for lane in range(2):
            c0, c1, c2 = p.index(lane)
            for copy in self.second[lane]:
                copy.wait_recv()
            for b in range(2):
                self.core.append(self.swap(piece_rows(c0, 1 - c1, b, lane), 0))

    def finish(self):
        for copy in self.core:
            copy.wait_recv()


def kernel(
    dp_size, shards,
    mol, fill, x, cot_in, gain_a, gain_f, qkv_in, wo_in, wu_in, wd_in,
    out_to, dtok_to, gains_out, up_to, down_to, own_to,
    wg, cot, wu, wd, f_ud, f_own,
    nw, xh, mask, qt, kt, vt, kn, vn, probs, share, mixf, mixt, dmt, dbr, dres,
    dqkv, dkt, dvt, halo_out, halo_in, g_ud, g_k, r0, r1, r2, rx, r_last, zud, zk,
    gain_sum, gain_got, gain_col,
    send_sem, recv_sem, halo_send, halo_recv, load_sem,
):
    place = Place(dp_size, shards)
    link = Link(send_sem, recv_sem)
    z = place.z
    last = shards - 1
    nffn, hidden, dinner, out = (g_k.at[i, pl.ds(0, ROWS)] for i in range(4))
    scale = HEAD_DIM ** (-0.5)
    width = dmt.shape[1]

    def column(k):
        return {"head": place.across(k)}

    moves = []

    def move(src, dst):
        copy = pltpu.make_async_copy(src, dst, load_sem.at[len(moves)])
        copy.start()
        moves.append(copy)
        return copy

    own_w = [
        move(qkv_in, wg.at[z, pl.ds(0, 3 * width)]),
        move(wo_in, wg.at[z, pl.ds(3 * width, width)]),
    ]
    ffn_w = [move(wu_in, wu), move(wd_in, wd), move(cot_in, cot)]

    barrier = pltpu.get_barrier_semaphore()
    peers = [place.near(b) for b in range(len(place.bits))] + [column(k) for k in range(1, shards)]
    for peer in peers:
        pl.semaphore_signal(barrier, inc=1, device_id=peer, device_id_type=MESH)
    pl.semaphore_wait(barrier, len(peers))

    after = {"head": jnp.minimum(z + 1, last)}
    before = {"head": jnp.maximum(z - 1, 0)}
    to_next = link.make(x.at[pl.ds(ROWS - SLOT, SLOT)], xh.at[0], after)
    to_prev = link.make(x.at[pl.ds(0, SLOT)], xh.at[1], before)

    for copy in own_w:
        copy.wait()
    lanes = [piece_rows(*place.index(lane), lane) for lane in range(2)]
    inner = (z > 0) & (z < last)
    outer = (z == 0) | (z == last)
    near_z = [place.across(1), 2 - z // 2, last - last * (z // 2)]
    line = link.reserve(max(10, 2 * shards))
    passed = []

    def along(g, target, step):
        return [
            pltpu.make_async_remote_copy(
                src_ref=wg.at[g, rows], dst_ref=wg.at[g, rows],
                send_sem=send_sem.at[line + 2 * step + lane], recv_sem=recv_sem.at[line + 2 * g + lane],
                device_id={"head": target}, device_id_type=MESH,
            )
            for lane, rows in enumerate(lanes)
        ]

    def pass_on(keep, g, target, step):
        copies = along(g, target, step)
        passed.append((keep, copies))

        @pl.when(keep)
        def _():
            for copy in copies:
                copy.start()

    def arrived(g):
        for copy in along(g, after["head"], 0):
            copy.wait_recv()

    pass_on(z < last, z, after["head"], 0)
    pass_on(z > 0, z, before["head"], 1)
    spread = [None] + [Spread(link, place, wg.at[g]) for g in near_z]

    def pick_up(step):
        first, second, third = near_z
        if step == 1:
            arrived(first)
            pass_on(inner, first, last - z, 2)

            @pl.when(inner)
            def _():
                arrived(second)

            pass_on(inner, second, last * (z // 2), 3)
        if step == 2:

            @pl.when(outer)
            def _():
                arrived(second)

            @pl.when(inner)
            def _():
                arrived(third)

            pass_on(inner, third, last * (z // 2), 4)
        if step == 3:

            @pl.when(outer)
            def _():
                arrived(third)

        spread[step].start()

    build_masks(mask, width)
    extend(fill, z, width, qt, kt, vt, kn, vn)

    def normed(at_w, ref, at):
        zz, _ = norm_stats(ref[at, :].astype(F32))
        nw[at_w, :] = (zz * gain_a[...].reshape(1, D)).astype(BF)

    @pl.loop(0, ROWS // 64)
    def _(i):
        at = pl.multiple_of(i * 64, 64)
        normed(pl.ds(at + SLOT, 64), x, pl.ds(at, 64))

    @pl.when(z < last)
    def _():
        to_next.start()

    @pl.when(z > 0)
    def _():
        to_prev.start()

    def weight(g, c):
        return wg[g, c * width : (c + 1) * width, :]

    def heads_mix(g, low, high, step=1):
        @pl.loop(0, (high - low) // step)
        def _(i):
            s = low + i * step
            attend(g, s, slot_meta(mol, z, s), mask, qt, kn, vt, probs, share, mixf, mixt)

    project(z, [weight(z, c) for c in range(3)], nw, SLOT, ROWS, qt, kt, vt, kn, vn, scale)
    heads_mix(z, 1, SLOTS_DEV - 1)
    pick_up(1)

    @pl.when(z > 0)
    def _():
        to_next.wait_recv()

    @pl.when(z == 0)
    def _():
        xh[0] = jnp.zeros_like(xh[0])

    @pl.when(z < last)
    def _():
        to_prev.wait_recv()

    @pl.when(z == last)
    def _():
        xh[1] = jnp.zeros_like(xh[1])

    @pl.loop(0, SLOT // 64)
    def _(i):
        at = pl.multiple_of(i * 64, 64)
        normed(pl.ds(at, 64), xh.at[0], pl.ds(at, 64))
        normed(pl.ds(at + SLOT + ROWS, 64), xh.at[1], pl.ds(at, 64))

    for low in (0, SLOT + ROWS):
        project(z, [None, weight(z, 1), weight(z, 2)], nw, low, SLOT, qt, kt, vt, kn, vn, scale)
    spread[1].step1()
    pick_up(2)
    heads_mix(z, 0, 2 * (SLOTS_DEV - 1), SLOTS_DEV - 1)

    def heads_in(g):
        project(g, [weight(g, c) for c in range(3)], nw, 0, WIN, qt, kt, vt, kn, vn, scale)

    spread[1].step2()
    spread[2].step1()
    pick_up(3)
    spread[1].finish()
    heads_in(near_z[0])
    spread[2].step2()
    spread[3].step1()
    heads_mix(near_z[0], 0, SLOTS_DEV)
    spread[2].finish()
    spread[3].step2()
    heads_in(near_z[1])
    heads_mix(near_z[1], 0, SLOTS_DEV)
    spread[3].finish()
    heads_in(near_z[2])
    heads_mix(near_z[2], 0, SLOTS_DEV)

    mixn = mixt[...].T
    total = x[...].astype(F32)
    for g in range(shards):
        total = total + nn(mixn[:, g * width : (g + 1) * width], weight(g, 3))
    dres[...] = total

    gain_sum[...] = jnp.zeros_like(gain_sum)

    @pl.loop(0, ROWS // 64)
    def _(i):
        at = pl.ds(pl.multiple_of(i * 64, 64), 64)
        zz, _ = norm_stats(dres[at, :])
        nffn[at, :] = (zz * gain_f[...].reshape(1, D)).astype(BF)

    BLK = 256
    for copy in ffn_w:
        copy.wait()

    @pl.loop(0, ROWS // BLK)
    def _(i):
        at = pl.ds(pl.multiple_of(i * BLK, BLK), BLK)
        u = nn(nffn[at, :], wu[...])
        c = cot[at, :]
        dh = nt(c, wd[...])
        cdf = 0.5 + 0.5 * lax.erf(u * SQH)
        h = (u * cdf).astype(BF)
        hidden[at, :] = h
        dinner[at, :] = (dh * (cdf + u * (PHI * jnp.exp(-0.5 * u * u)))).astype(BF)
        out[at, :] = (dres[at, :] + nn(h, wd[...])).astype(BF)

    out_move = move(out, out_to)
    g_ud[1] = tn(hidden[...], cot[...]).astype(BF)
    down = Halve(link, place, g_ud.at[1], *(r.at[shards + 1] for r in (r0, r1, r2, rx)))
    down.start()
    g_ud[0] = tn(nffn[...], dinner[...]).astype(BF)
    up = Halve(link, place, g_ud.at[0], *(r.at[shards] for r in (r0, r1, r2, rx)))
    up.start()
    down.step1()

    @pl.loop(0, ROWS // BLK)
    def _(i):
        at = pl.ds(pl.multiple_of(i * BLK, BLK), BLK)
        dn = nt(dinner[at, :], wu[...])
        zz, r = norm_stats(dres[at, :])
        gain_sum[1:2, :] += jnp.sum(dn * zz, axis=0, keepdims=True)
        dr = cot[at, :].astype(F32) + norm_back(dn, zz, r, gain_f[...].reshape(1, D))
        dres[at, :] = dr
        dbr[at, :] = dr.astype(BF)

    up.step1()
    dkt[...] = jnp.zeros_like(dkt)
    dvt[...] = jnp.zeros_like(dvt)

    def back(g, s):
        attend_back(
            g, s, slot_meta(mol, z, s), mask, qt, kt, vn, dmt, probs, share, mixf, dqkv, dkt, dvt, scale
        )

    def halo_copy(side, g):
        return pltpu.make_async_remote_copy(
            src_ref=halo_out.at[side, g], dst_ref=halo_in.at[side, g],
            send_sem=halo_send.at[side, g], recv_sem=halo_recv.at[side, g],
            device_id=after if side else before, device_id_type=MESH,
        )

    def border(g):
        dmt[g] = nt(wg[g, 3 * width : 4 * width, :], dbr[...]).astype(BF)

        @pl.loop(0, 2)
        def _(i):
            back(g, i * (SLOTS_DEV - 1))

        for side, cols in ((0, slice(0, SLOT)), (1, slice(SLOT + ROWS, WIN))):
            halo_out[side, g, 0] = dkt[g, :, cols].astype(BF)
            halo_out[side, g, 1] = dvt[g, :, cols].astype(BF)

        @pl.when(z > 0)
        def _():
            halo_copy(0, g).start()

        @pl.when(z < last)
        def _():
            halo_copy(1, g).start()

    def middle(g):
        @pl.loop(1, SLOTS_DEV - 1)
        def _(s):
            back(g, s)

    def shard_grads(k, g):
        @pl.when(z < last)
        def _():
            halo_copy(0, g).wait_recv()
            cols = slice(ROWS, SLOT + ROWS)
            dkt[g, :, cols] += halo_in[0, g, 0].astype(F32)
            dvt[g, :, cols] += halo_in[0, g, 1].astype(F32)

        @pl.when(z > 0)
        def _():
            halo_copy(1, g).wait_recv()
            cols = slice(SLOT, 2 * SLOT)
            dkt[g, :, cols] += halo_in[1, g, 0].astype(F32)
            dvt[g, :, cols] += halo_in[1, g, 1].astype(F32)

        dqkv[g, 1] = dkt[g, :, SLOT : SLOT + ROWS].astype(BF)
        dqkv[g, 2] = dvt[g, :, SLOT : SLOT + ROWS].astype(BF)
        own = nw[SLOT : SLOT + ROWS, :]
        for c in range(3):
            g_k[k, c * width : (c + 1) * width, :] = nn(dqkv[g, c], own).astype(BF)
        at = pl.ds(pl.multiple_of(g * width, 16), width)
        g_k[k, 3 * width : 4 * width, :] = nn(mixt[at, :], dbr[...]).astype(BF)
        job = Halve(link, place, *(r.at[k] for r in (g_k, r0, r1, r2, rx)))
        job.start()
        return job

    def quarter(ref, q):
        lane = q % 2
        c0, ca, cb = place.index(0)
        rows = piece_rows(c0, ca + lane * (cb - ca), cb + lane * (ca - cb), lane)
        return ref.at[rows, pl.ds(pl.multiple_of(q // 2 * (D // 2), 128), D // 2)]

    class Column:
        def __init__(self, i):
            self.g, self.got, self.f, self.spread = g_ud.at[i], zud.at[i], f_ud.at[i], Spread(link, place, f_ud.at[i])

        def send(self):
            self.copies = [
                link.send(quarter(self.g, place.across(k)), self.got.at[k - 1], column(k)) for k in range(1, shards)
            ]

        def sum(self):
            for copy in self.copies:
                copy.wait_recv()
            mine, dst = quarter(self.g, z), quarter(self.f, z)
            add_rows(mine, *[self.got.at[k] for k in range(shards - 1)])
            dst[...] = mine[...]
            self.copies = [link.send(dst, dst, column(k)) for k in range(1, shards)]

        def start(self):
            for copy in self.copies:
                copy.wait_recv()
            self.spread.start()

    up_z, down_z = Column(0), Column(1)
    own_spread = Spread(link, place, f_own)

    upper = (z * 2) // shards
    turn = [1 + upper, 2 + upper, 3 - 2 * upper]
    z_slot = link.reserve(2 * (shards - 1))

    def z_copy(k, lane, src):
        return link.make(src, zk.at[k - 1, lane], column(k), z_slot + 2 * (k - 1) + lane)

    def send_shard(i, job):
        for lane in range(2):
            copy = z_copy(turn[i], lane, job.mine(lane))
            copy.start()
            link.open.append(copy)

    g1, g2, g3 = (place.across(k) for k in turn)
    border(0)
    down.step2()
    border(1)
    up.step2()
    middle(g1)
    down.step3()
    down_z.send()
    job1 = shard_grads(1, g1)
    up.step3()
    up_z.send()
    border(2)
    job1.step1()
    border(3)
    down_z.sum()
    middle(g2)
    job1.step2()
    up_z.sum()
    job2 = shard_grads(2, g2)
    middle(g3)
    job2.step1()
    job1.step3()
    send_shard(0, job1)
    down_z.start()
    out_move.wait()
    job3 = shard_grads(3, g3)
    up_z.start()
    middle(z)
    job3.step1()
    job2.step2()
    down_z.spread.step1()
    job0 = shard_grads(0, z)

    def tokens_back(low, size):
        at = slice(low, low + size)
        dn = tn(
            dqkv[:, :, :, at].reshape(shards * 3 * width, size),
            jnp.concatenate([wg[g, : 3 * width, :] for g in range(shards)], axis=0),
        )
        zz, r = norm_stats(x[at, :].astype(F32))
        gain_sum[0:1, :] += jnp.sum(dn * zz, axis=0, keepdims=True)
        dres[at, :] = dres[at, :] + norm_back(dn, zz, r, gain_a[...].reshape(1, D))

    tokens_back(0, BLK // 2)
    job0.step1()
    up_z.spread.step1()
    down_z.spread.step2()
    job3.step2()
    tokens_back(BLK // 2, BLK)
    job2.step3()
    send_shard(1, job2)
    job3.step3()
    send_shard(2, job3)
    up_z.spread.step2()
    tokens_back(BLK // 2 + BLK, BLK // 2)
    move(dres, dtok_to)

    def gain_swap(bit):
        return link.send(gain_sum, gain_got.at[bit], place.near(bit))

    def gain_add(bit, copy):
        copy.wait_recv()
        link.done(copy)
        gain_sum[...] += gain_got[bit]

    def own_sum(lane):
        mine = job0.mine(lane)
        for k in range(1, shards):
            z_copy(k, lane, mine).wait_recv()
        add_rows(mine, *[zk.at[k, lane] for k in range(shards - 1)])

    swapped = gain_swap(0)
    if len(place.bits) == HALVINGS:
        job0.step2(own_sum, r_last)
        gain_add(0, swapped)
        swapped = gain_swap(1)
        down_z.spread.finish()
        up_z.spread.finish()
        move(f_ud.at[0], up_to)
        move(f_ud.at[1], down_to)
        gain_add(1, swapped)
        swapped = gain_swap(2)
        job0.step3_both(r_last, own_spread)
        gain_add(2, swapped)
    else:
        job0.step2()
        gain_add(0, swapped)
        for bit in range(1, len(place.bits)):
            gain_add(bit, gain_swap(bit))
        down_z.spread.finish()
        up_z.spread.finish()
        move(f_ud.at[0], up_to)
        move(f_ud.at[1], down_to)
        job0.step3()
        for lane in range(2):
            own_sum(lane)
            f_own.at[piece_rows(*place.index(lane), lane)][...] = job0.mine(lane)[...]
        own_spread.start()
        own_spread.step1()
    gain_col[z] = gain_sum[...]
    gain_copies = [link.send(gain_sum, gain_col.at[z], column(k)) for k in range(1, shards)]
    own_spread.step2()
    for copy in gain_copies:
        copy.wait_recv()
    gains_out[...] = sum(gain_col[k] for k in range(shards))
    own_spread.finish()
    move(f_own, own_to)

    link.drain()
    for keep, copies in passed:

        @pl.when(keep)
        def _():
            for copy in copies:
                copy.wait_send()

    @pl.when(z < last)
    def _():
        to_next.wait_send()
        for g in range(shards):
            halo_copy(1, g).wait_send()

    @pl.when(z > 0)
    def _():
        to_prev.wait_send()
        for g in range(shards):
            halo_copy(0, g).wait_send()

    for copy in moves[len(own_w + ffn_w) + 1 :]:
        copy.wait()


VM = pl.BlockSpec(memory_space=pltpu.VMEM)
SM = pl.BlockSpec(memory_space=pltpu.SMEM)
ANY = pl.BlockSpec(memory_space=pl.ANY)
COPIES = 224


def S(shape, dtype):
    return jax.ShapeDtypeStruct(shape, dtype)


def layer(dp_size, n, width, *operands):
    pairs = width // (2 * HEAD_DIM)
    step = 8
    more = 0
    while step < dp_size:
        step *= 2
        more += 1
    extra = max(more, 1)
    bits = 3 + more
    V = pltpu.VMEM
    return pl.pallas_call(
        functools.partial(kernel, dp_size, n),
        out_shape=(
            S((ROWS, D), BF), S((ROWS, D), F32), S((8, D), F32), S((D, D), BF), S((D, D), BF), S((D, D), BF),
        ),
        in_specs=[SM, SM, VM, ANY, VM, VM] + [ANY] * 4,
        out_specs=(ANY, ANY, VM, ANY, ANY, ANY),
        scratch_shapes=[
            V((n, D, D), BF),
            V((ROWS, D), BF),
            V((D, D), BF),
            V((D, D), BF),
            V((2, D, D), BF),
            V((D, D), BF),
            V((WIN, D), BF),
            V((2, SLOT, D), BF),
            V((pairs, width + WIDER, 2 * SLOT), BF),
            V((n, width + WIDER, ROWS), BF),
            V((n, width, WIN), BF),
            V((n, width, WIN), BF),
            V((n, WIN + SLOT, width + WIDER), BF),
            V((n, WIN, width + WIDER), BF),
            V((n, SLOTS_DEV, pairs, 2 * SLOT, 2 * SLOT), BF),
            V((n, width, ROWS), F32),
            V((n, width, ROWS), F32),
            V((D, ROWS), BF),
            V((n, width, ROWS), BF),
            V((ROWS, D), BF),
            V((ROWS, D), F32),
            V((n, 3, width, ROWS), BF),
            V((n, width, WIN), F32),
            V((n, width, WIN), F32),
            V((2, n, 2, width, SLOT), BF),
            V((2, n, 2, width, SLOT), BF),
            V((2, D, D), BF),
            V((n, D, D), BF),
            V((n + 2, D // 2, D), BF),
            V((n + 2, 2, 2, LANE, D), BF),
            V((n + 2, 2, LANE, D), BF),
            V((n + 2, extra, 2, LANE, D), BF),
            V((2, 2, LANE, D), BF),
            V((2, n - 1, LANE, D // 2), BF),
            V((n - 1, 2, LANE, D), BF),
            V((8, D), F32),
            V((bits, 8, D), F32),
            V((n, 8, D), F32),
            pltpu.SemaphoreType.DMA((COPIES + 12 * more,)),
            pltpu.SemaphoreType.DMA((COPIES + 12 * more,)),
            pltpu.SemaphoreType.DMA((2, n)),
            pltpu.SemaphoreType.DMA((2, n)),
            pltpu.SemaphoreType.DMA((16,)),
        ],
        compiler_params=pltpu.CompilerParams(
            vmem_limit_bytes=67043328, collective_id=0, has_side_effects=True
        ),
        name="layer",
    )(*operands)


CHUNK = 128


def finish_kernel(width, out, dtok, gains, up, down, own, *refs):
    outs, (out_v, dtok_v, raw, wide, in_sem, out_sem) = refs[:8], refs[8:]
    out_to, dtok_to, gain_a_to, gain_f_to, qkv_to, wo_to, up_to, down_to = outs
    parts = [(up, up_to, i, i) for i in range(0, D, CHUNK)] + [(down, down_to, i, i) for i in range(0, D, CHUNK)]
    size = CHUNK // 2
    small = [(own, qkv_to, i, i) for i in range(0, 3 * width, size)]
    small += [(own, wo_to, 3 * width + i, i) for i in range(0, width, size)]
    jobs = [(a, b, i, j, CHUNK) for a, b, i, j in parts] + [(a, b, i, j, size) for a, b, i, j in small]
    loads, at = [], 0
    for n, (src, _, i, _, rows) in enumerate(jobs):
        copy = pltpu.make_async_copy(src.at[pl.ds(i, rows)], raw.at[pl.ds(at, rows)], in_sem.at[n])
        copy.start()
        loads.append(copy)
        at += rows
    through = []
    for n, (src, mid, dst) in enumerate(((dtok, dtok_v, dtok_to), (out, out_v, out_to))):
        first = pltpu.make_async_copy(src, mid, in_sem.at[len(jobs) + n])
        first.start()
        through.append((first, pltpu.make_async_copy(mid, dst, out_sem.at[len(jobs) + n])))
    gain_a_to[...] = gains[0, :]
    gain_f_to[...] = gains[1, :]
    stores, at = [], 0
    for n, (_, dst, _, j, rows) in enumerate(jobs):
        loads[n].wait()

        @pl.loop(0, rows // 16)
        def _(i):
            rows16 = pl.ds(pl.multiple_of(at + i * 16, 16), 16)
            wide[rows16, :] = raw[rows16, :].astype(F32)

        copy = pltpu.make_async_copy(wide.at[pl.ds(at, rows)], dst.at[pl.ds(j, rows)], out_sem.at[n])
        copy.start()
        stores.append(copy)
        at += rows
    for first, second in through:
        first.wait()
        second.start()
        stores.append(second)
    for copy in stores:
        copy.wait()


def finish(width, *operands):
    V = pltpu.VMEM
    sems = pltpu.SemaphoreType.DMA((2 * D // CHUNK + 2 * D // CHUNK + 2,))
    return pl.pallas_call(
        functools.partial(finish_kernel, width),
        out_shape=(
            S((ROWS, D), BF), S((ROWS, D), F32), S((D,), F32), S((D,), F32),
            S((3 * width, D), F32), S((width, D), F32), S((D, D), F32), S((D, D), F32),
        ),
        in_specs=[ANY, ANY, VM, ANY, ANY, ANY],
        out_specs=(ANY, ANY, VM, VM, ANY, ANY, ANY, ANY),
        scratch_shapes=[V((ROWS, D), BF), V((ROWS, D), F32), V((3 * D, D), BF), V((3 * D, D), F32), sems, sems],
        name="finish",
    )(*operands)


def local(tokens_in, gain_attn, gain_ffn, w_qkv, w_out, w_up, w_down, slot_mol, slot_fill, cotangent):
    n = lax.axis_size("head")
    width = w_out.shape[0]
    results = layer(
        lax.axis_size("dp"), n, width,
        slot_mol, slot_fill, tokens_in, cotangent, gain_attn, gain_ffn,
        w_qkv.transpose(0, 2, 1).reshape(3 * width, D), w_out, w_up, w_down,
    )
    out, dtok, d_gain_a, d_gain_f, d_qkv, d_wo, d_up, d_down = finish(width, *results)
    return (
        out, dtok, d_gain_a, d_gain_f, d_qkv.reshape(3, width, D).transpose(0, 2, 1), d_wo, d_up, d_down,
    )


def solution(mesh):
    return jax.shard_map(
        local,
        mesh=mesh,
        in_specs=(
            P(("dp", "head"), None), P(), P(), P(None, None, "head"), P("head", None), P(), P(),
            P("dp", None), P("dp", None), P(("dp", "head"), None),
        ),
        out_specs=(
            P(("dp", "head"), None), P(("dp", "head"), None), P(), P(), P(None, None, "head"), P("head", None), P(), P(),
        ),
        check_vma=False,
    )
```

```python
import functools

import jax
import jax.numpy as jnp
from jax import lax
from jax.experimental import pallas as pl
from jax.experimental.pallas import tpu as pltpu
from jax.sharding import PartitionSpec as P

HEAD_DIM = 24
SLOT = 128
D = 768
EPS = 1e-05
SLOTS_DEV = 4
ROWS = SLOTS_DEV * SLOT
WIN = ROWS + 2 * SLOT
BF = jnp.bfloat16
F32 = jnp.float32


def nn(a, b):
    return jnp.dot(a, b, preferred_element_type=F32)


def nt(a, b):
    return lax.dot_general(a, b, (((1,), (1,)), ((), ())), preferred_element_type=F32)


def tn(a, b):
    return lax.dot_general(a, b, (((0,), (0,)), ((), ())), preferred_element_type=F32)


def norm_stats(v):
    mean = jnp.mean(v, axis=-1, keepdims=True)
    centred = v - mean
    var = jnp.mean(centred * centred, axis=-1, keepdims=True)
    r = lax.rsqrt(var + EPS)
    return centred * r, r


def norm_back(grad, z, r, gain):
    e = grad * gain
    return r * (e - jnp.mean(e, -1, keepdims=True) - z * jnp.mean(e * z, -1, keepdims=True))


WIDER = 64


def build_masks(mask_ref, width):
    shape = mask_ref.shape[1:]
    rows = lax.broadcasted_iota(jnp.int32, shape, 0)
    right = (lax.broadcasted_iota(jnp.int32, shape, 1) >= SLOT).astype(jnp.int32)
    for p in range(mask_ref.shape[0]):
        low = (2 * p + right) * HEAD_DIM
        keep = ((rows >= low) & (rows < low + HEAD_DIM)) | (rows >= width)
        mask_ref[p] = jnp.where(keep, 1.0, 0.0).astype(BF)


def extend(fill_ref, z, width, qt, kt, vt, kn, vn):
    lane = lax.broadcasted_iota(jnp.int32, (SLOT, WIDER), 1)
    row = lax.broadcasted_iota(jnp.int32, (SLOT, WIDER), 0)
    ones = jnp.where(lane < 2, 1.0, 0.0).astype(BF)
    top = lax.broadcasted_iota(jnp.int32, (WIDER, ROWS), 0)
    first = jnp.where(top == 0, 1.0, 0.0).astype(BF)
    slots = (WIN + SLOT) // SLOT
    for g in range(qt.shape[0]):
        qt[g, width:, :] = first
        kn[g, WIN:, :width] = jnp.zeros((SLOT, width), BF)
    for s in range(slots):
        live = 0
        if s < slots - 1:
            at = jnp.minimum(jnp.maximum(z * SLOTS_DEV + s - 1, 0), fill_ref.shape[1] - 1)
            live = fill_ref[0, at]
        bias = jnp.where((lane == 0) & (row >= live), -1e30, 0.0).astype(BF)
        for g in range(qt.shape[0]):
            kn[g, s * SLOT : (s + 1) * SLOT, width:] = bias
            if s < slots - 1:
                vn[g, s * SLOT : (s + 1) * SLOT, width:] = ones


def slot_meta(mol_ref, z, s):
    at = z * SLOTS_DEV + s
    last = mol_ref.shape[1] - 1
    before, after = jnp.maximum(at - 1, 0), jnp.minimum(at + 1, last)
    mine = mol_ref[0, at]
    prev = jnp.where((mol_ref[0, before] == mine) & (at > 0), 1, 0)
    nxt = jnp.where((mol_ref[0, after] == mine) & (at < last), 1, 0)
    return prev, nxt * (1 - prev)


def chosen(*terms):
    total = None
    for flag, block in terms:
        term = jnp.broadcast_to(flag.astype(F32), block.shape).astype(BF) * block
        total = term if total is None else total + term
    return total


def pair_rows(full):
    rows = lax.broadcasted_iota(jnp.int32, (2 * HEAD_DIM, SLOT), 0)
    return jnp.where(rows < HEAD_DIM, full[:, :SLOT], full[:, SLOT:])


def project(g, parts, nw, low, count, qt, kt, vt, kn, vn, scale):
    width = kt.shape[1]
    at = slice(low, low + count)
    if parts[0] is not None:
        qt[g, :width, :] = (nt(parts[0], nw[pl.ds(SLOT, ROWS), :]) * scale).astype(BF)
    for part, wide, tall in ((parts[1], kt, kn), (parts[2], vt, vn)):
        rows = nt(part, nw[at, :]).astype(BF)
        wide[g, :, at] = rows
        tall[g, at, :width] = rows.T


def windows(s):
    own = pl.multiple_of((s + 1) * SLOT, SLOT)
    before = pl.multiple_of(s * SLOT, SLOT)
    after = pl.multiple_of((s + 2) * SLOT, SLOT)
    return pl.ds(own, SLOT), pl.ds(before, SLOT), pl.ds(after, SLOT), pl.ds(before, SLOT)


def attend(g, s, meta, mask, qt, kn, vt, probs, share, mixf, mixt, room):
    prev, nxt = meta
    own, before, after, mine = windows(s)
    width = vt.shape[1]
    partner = chosen((prev, kn[g, before, :]), (nxt, kn[g, after, :]), (1 - prev - nxt, kn[g, WIN:, :]))
    keys = jnp.concatenate([kn[g, own, :], partner], axis=0)
    vals = jnp.concatenate([vt[g, :, own], chosen((prev, vt[g, :, before]), (nxt, vt[g, :, after]))], axis=1)
    ones = jnp.ones((16, 2 * SLOT), BF)
    q = qt[g, :, mine]
    q2 = jnp.concatenate([q, q], axis=1)
    pairs = mask.shape[0]
    left, right = slice(0, 2 * SLOT), slice(2 * SLOT, 4 * SLOT)
    tops = [None] * pairs

    def score(p):
        scores = nn(keys, q2 * mask[p])
        room[p, :SLOT, left] = scores[:SLOT]
        room[p, :SLOT, right] = scores[SLOT:]
        tops[p] = jnp.max(scores, axis=0, keepdims=True)

    def weigh(p):
        probs[g, s, p, :SLOT, :] = jnp.exp(room[p, :SLOT, left] - tops[p]).astype(BF)
        probs[g, s, p, SLOT:, :] = jnp.exp(room[p, :SLOT, right] - tops[p]).astype(BF)

    def mix(p):
        head_rows = slice(2 * HEAD_DIM * p, 2 * HEAD_DIM * (p + 1))
        both = nn(jnp.concatenate([vals[head_rows, :], ones], axis=0), probs[g, s, p])
        part = pair_rows(jnp.broadcast_to(1.0 / both[2 * HEAD_DIM : 2 * HEAD_DIM + 1, :], (2 * HEAD_DIM, 2 * SLOT)))
        mixed = pair_rows(both[: 2 * HEAD_DIM, :]) * part
        share[g, head_rows, mine] = part
        mixf[g, head_rows, mine] = mixed
        at = pl.ds(pl.multiple_of(g * width + 2 * HEAD_DIM * p, 16), 2 * HEAD_DIM)
        mixt[at, mine] = mixed.astype(BF)

    for step in range(pairs + 4):
        if step < pairs:
            score(step)
        if 0 <= step - 2 < pairs:
            weigh(step - 2)
        if 0 <= step - 4 < pairs:
            mix(step - 4)


def attend_back(g, s, meta, mask, qt, kt, vn, dmt, probs, share, mixf, dqkv, dkt, dvt, scale, room):
    prev, nxt = meta
    own, before, after, mine = windows(s)
    width = dmt.shape[1]
    fprev, fnext = prev.astype(F32), nxt.astype(F32)
    vals = jnp.concatenate([vn[g, own, :], chosen((prev, vn[g, before, :]), (nxt, vn[g, after, :]))], axis=0)
    keys = jnp.concatenate([kt[g, :, own], chosen((prev, kt[g, :, before]), (nxt, kt[g, :, after]))], axis=1)
    q = qt[g, :width, mine]
    dm = (dmt[g, :, mine].astype(F32) * share[g, :, mine]).astype(BF)
    q2 = jnp.concatenate([q, q], axis=1)
    dm2 = jnp.concatenate([dm, dm], axis=1)
    prod = dm.astype(F32) * mixf[g, :, mine]
    line = lax.broadcasted_iota(jnp.int32, (16, 2 * SLOT), 0)
    rest = jnp.zeros((WIDER - 16, 2 * SLOT), BF)
    pairs = mask.shape[0]
    kept = [None] * pairs

    def rows_of(p):
        return slice(2 * HEAD_DIM * p, 2 * HEAD_DIM * (p + 1))

    def place_of(p):
        return room.at[pl.ds(p // 3 * 2 * SLOT, 2 * SLOT), pl.ds(p % 3 * 2 * SLOT, 2 * SLOT)]

    def slopes(p):
        mid = 2 * HEAD_DIM * p + HEAD_DIM
        inner = jnp.concatenate(
            [
                jnp.sum(prod[2 * HEAD_DIM * p : mid], axis=0, keepdims=True),
                jnp.sum(prod[mid : mid + HEAD_DIM], axis=0, keepdims=True),
            ],
            axis=1,
        )
        high = inner.astype(BF).astype(F32)
        take_off = jnp.where(line == 0, -high, jnp.where(line == 1, high - inner, 0.0)).astype(BF)
        rhs = dm2 * mask[p, :width, :]
        d_probs = nn(vals, jnp.concatenate([rhs, take_off, rest], axis=0))
        place_of(p)[...] = probs[g, s, p] * d_probs.astype(BF)
        kept[p] = nt(rhs[rows_of(p), :], probs[g, s, p])

    def pull(p):
        head_rows = rows_of(p)
        d_scores = place_of(p)[...]
        dq = pair_rows(nn(keys[head_rows, :], d_scores)) * scale
        dqkv[g, 0, head_rows, mine] = dq.astype(BF)
        qm = (q2 * mask[p, :width, :])[head_rows, :]
        dk = nt(qm, d_scores)
        dv = kept[p]
        dkt[g, head_rows, own] += dk[:, :SLOT]
        dvt[g, head_rows, own] += dv[:, :SLOT]
        dkt[g, head_rows, before] += fprev * dk[:, SLOT:]
        dvt[g, head_rows, before] += fprev * dv[:, SLOT:]
        dkt[g, head_rows, after] += fnext * dk[:, SLOT:]
        dvt[g, head_rows, after] += fnext * dv[:, SLOT:]

    for step in range(pairs + 2):
        if step < pairs:
            slopes(step)
        if step >= 2:
            pull(step - 2)


SQH = 0.7071067811865476
PHI = 0.3989422804014327
MESH = pl.DeviceIdType.MESH
HALVINGS = 3
PIECE = D // 8
LANE = PIECE // 2


class Link:
    def __init__(self, send_sem, recv_sem):
        self.send_sem, self.recv_sem, self.used, self.open = send_sem, recv_sem, 0, []

    def reserve(self, count):
        self.used += count
        return self.used - count

    def make(self, src, dst, target, slot=None):
        slot = self.reserve(1) if slot is None else slot
        return pltpu.make_async_remote_copy(
            src_ref=src, dst_ref=dst, send_sem=self.send_sem.at[slot], recv_sem=self.recv_sem.at[slot],
            device_id=target, device_id_type=MESH,
        )

    def send(self, src, dst, target):
        copy = self.make(src, dst, target)
        copy.start()
        self.open.append(copy)
        return copy

    def done(self, copy):
        copy.wait_send()
        self.open = [c for c in self.open if c is not copy]

    def drain(self):
        for copy in self.open:
            copy.wait_send()
        self.open = []


def add_rows(dst, *terms):
    @pl.loop(0, dst.shape[0] // 16)
    def _(i):
        at = pl.ds(pl.multiple_of(i * 16, 16), 16)
        total = dst[at, :].astype(F32)
        for term in terms:
            total = total + term[at, :].astype(F32)
        dst[at, :] = total.astype(dst.dtype)


def piece_rows(d0, d1, d2, lane):
    return pl.ds(pl.multiple_of(((d0 * 2 + d1) * 2 + d2) * PIECE + lane * LANE, 16), LANE)


class Place:
    def __init__(self, dp_size, shards):
        self.dp = lax.axis_index("dp")
        self.z = lax.axis_index("head")
        self.shards = shards
        self.bits, self.partner = [], []
        step = 1
        while step < dp_size:
            bit = (self.dp // step) % 2
            self.bits.append(bit)
            self.partner.append(self.dp + step - 2 * step * bit)
            step *= 2
        self.order = ((0, 1, 2), (0, 2, 1))

    def near(self, bit):
        return {"dp": self.partner[bit]}

    def across(self, k):
        step, found = 1, 0
        while step < self.shards:
            found = found + step * ((self.z // step + k // step) % 2)
            step *= 2
        return found

    def index(self, lane):
        return tuple(self.bits[b] for b in self.order[lane])


class Halve:
    def __init__(self, link, place, g, r0, r1, r2, rx):
        self.link, self.place, self.g, self.r0, self.r1, self.r2, self.rx = link, place, g, r0, r1, r2, rx

    def start(self):
        p = self.place
        self.pass_on, self.keep = [], []
        for side, out in ((1, self.pass_on), (0, self.keep)):
            for lane in range(2):
                c0, c1, _ = p.index(lane)
                d1 = c1 + side * (1 - 2 * c1)
                out.append(
                    [
                        self.link.send(
                            self.g.at[piece_rows(1 - c0, d1, b, lane)], self.r0.at[piece_rows(0, d1, b, lane)], p.near(0)
                        )
                        for b in range(2)
                    ]
                )

    def mine(self, lane):
        return self.g.at[piece_rows(*self.place.index(lane), lane)]

    def step1(self):
        p = self.place
        self.copies = []
        for lane in range(2):
            c0, c1, _ = p.index(lane)
            sent = []
            for b in range(2):
                self.pass_on[lane][b].wait_recv()
                part = self.g.at[piece_rows(c0, 1 - c1, b, lane)]
                add_rows(part, self.r0.at[piece_rows(0, 1 - c1, b, lane)])
                sent.append(self.link.send(part, self.r1.at[lane, b], p.near(p.order[lane][1])))
            self.copies.append(sent)

    def step2(self):
        p = self.place
        old, self.copies = self.copies, []
        for lane in range(2):
            c0, c1, c2 = p.index(lane)
            for b in range(2):
                self.keep[lane][b].wait_recv()
                old[lane][b].wait_recv()
            part = self.g.at[piece_rows(c0, c1, 1 - c2, lane)]
            add_rows(part, self.r0.at[piece_rows(0, c1, 1 - c2, lane)], self.r1.at[lane, 1 - c2])
            self.copies.append(self.link.send(part, self.r2.at[lane], p.near(p.order[lane][2])))

    def step3(self):
        p = self.place
        for lane in range(2):
            _, c1, c2 = p.index(lane)
            self.copies[lane].wait_recv()
            add_rows(self.mine(lane), self.r0.at[piece_rows(0, c1, c2, lane)], self.r1.at[lane, c2], self.r2.at[lane])
        for extra in range(HALVINGS, len(p.bits)):
            copies = [
                self.link.send(self.mine(lane), self.rx.at[extra - HALVINGS, lane], p.near(extra)) for lane in range(2)
            ]
            for lane in range(2):
                copies[lane].wait_recv()
                self.link.done(copies[lane])
                add_rows(self.mine(lane), self.rx.at[extra - HALVINGS, lane])


class Spread:
    def __init__(self, link, place, f):
        self.link, self.place, self.f = link, place, f

    def swap(self, rows, bit):
        part = self.f.at[rows]
        return self.link.send(part, part, self.place.near(bit))

    def begin(self):
        self.first, self.second, self.core = [], [[], []], []

    def pass_on(self, lane, rows):
        self.second[lane].append(self.swap(rows, self.place.order[lane][1]))
        self.core.append(self.swap(rows, 0))

    def start(self):
        p = self.place
        self.begin()
        for lane in range(2):
            own = piece_rows(*p.index(lane), lane)
            self.first.append(self.swap(own, p.order[lane][2]))
            self.pass_on(lane, own)

    def step1(self):
        p = self.place
        for lane in range(2):
            c0, c1, c2 = p.index(lane)
            self.first[lane].wait_recv()
            self.pass_on(lane, piece_rows(c0, c1, 1 - c2, lane))

    def step2(self):
        p = self.place
        for lane in range(2):
            c0, c1, c2 = p.index(lane)
            for copy in self.second[lane]:
                copy.wait_recv()
            for b in range(2):
                self.core.append(self.swap(piece_rows(c0, 1 - c1, b, lane), 0))

    def finish(self):
        for copy in self.core:
            copy.wait_recv()


def kernel(
    dp_size, shards,
    mol, fill, x, cot_in, gain_a, gain_f, qkv_in, wo_in, wu_in, wd_in,
    out_to, dtok_to, gains_out, up_to, down_to, own_to,
    wg, cot, wu, wd, f_ud, f_own,
    nw, xh, mask, qt, kt, vt, kn, vn, probs, share, mixf, mixt, dmt, dbr, dres,
    dqkv, dkt, dvt, halo_out, halo_in, g_ud, g_k, r0, r1, r2, rx, zud, zk,
    gain_sum, gain_got, gain_col,
    send_sem, recv_sem, halo_send, halo_recv, load_sem,
):
    place = Place(dp_size, shards)
    link = Link(send_sem, recv_sem)
    z = place.z
    last = shards - 1
    nffn, hidden, dinner, out = (g_k.at[i, pl.ds(0, ROWS)] for i in range(4))
    scale = HEAD_DIM ** (-0.5)
    width = dmt.shape[1]

    def column(k):
        return {"head": place.across(k)}

    moves = []

    def move(src, dst):
        copy = pltpu.make_async_copy(src, dst, load_sem.at[len(moves)])
        copy.start()
        moves.append(copy)
        return copy

    own_w = [
        move(qkv_in, wg.at[z, pl.ds(0, 3 * width)]),
        move(wo_in, wg.at[z, pl.ds(3 * width, width)]),
    ]
    ffn_w = [move(wu_in, wu), move(wd_in, wd), move(cot_in, cot)]

    barrier = pltpu.get_barrier_semaphore()
    peers = [place.near(b) for b in range(len(place.bits))] + [column(k) for k in range(1, shards)]
    for peer in peers:
        pl.semaphore_signal(barrier, inc=1, device_id=peer, device_id_type=MESH)
    pl.semaphore_wait(barrier, len(peers))

    after = {"head": jnp.minimum(z + 1, last)}
    before = {"head": jnp.maximum(z - 1, 0)}
    to_next = link.make(x.at[pl.ds(ROWS - SLOT, SLOT)], xh.at[0], after)
    to_prev = link.make(x.at[pl.ds(0, SLOT)], xh.at[1], before)

    for copy in own_w:
        copy.wait()
    lanes = [piece_rows(*place.index(lane), lane) for lane in range(2)]
    inner = (z > 0) & (z < last)
    outer = (z == 0) | (z == last)
    near_z = [place.across(1), 2 - z // 2, last - last * (z // 2)]
    line = link.reserve(max(10, 2 * shards))
    passed = []

    def along(g, target, step):
        return [
            pltpu.make_async_remote_copy(
                src_ref=wg.at[g, rows], dst_ref=wg.at[g, rows],
                send_sem=send_sem.at[line + 2 * step + lane], recv_sem=recv_sem.at[line + 2 * g + lane],
                device_id={"head": target}, device_id_type=MESH,
            )
            for lane, rows in enumerate(lanes)
        ]

    def pass_on(keep, g, target, step):
        copies = along(g, target, step)
        passed.append((keep, copies))

        @pl.when(keep)
        def _():
            for copy in copies:
                copy.start()

    def arrived(g):
        for copy in along(g, after["head"], 0):
            copy.wait_recv()

    pass_on(z < last, z, after["head"], 0)
    pass_on(z > 0, z, before["head"], 1)
    spread = [None] + [Spread(link, place, wg.at[g]) for g in near_z]

    def pick_up(step):
        first, second, third = near_z
        if step == 1:
            arrived(first)
            pass_on(inner, first, last - z, 2)

            @pl.when(inner)
            def _():
                arrived(second)

            pass_on(inner, second, last * (z // 2), 3)
        if step == 2:

            @pl.when(outer)
            def _():
                arrived(second)

            @pl.when(inner)
            def _():
                arrived(third)

            pass_on(inner, third, last * (z // 2), 4)
        if step == 3:

            @pl.when(outer)
            def _():
                arrived(third)

        spread[step].start()

    build_masks(mask, width)
    extend(fill, z, width, qt, kt, vt, kn, vn)

    def normed(at_w, ref, at):
        zz, _ = norm_stats(ref[at, :].astype(F32))
        nw[at_w, :] = (zz * gain_a[...].reshape(1, D)).astype(BF)

    @pl.loop(0, ROWS // 64)
    def _(i):
        at = pl.multiple_of(i * 64, 64)
        normed(pl.ds(at + SLOT, 64), x, pl.ds(at, 64))

    @pl.when(z < last)
    def _():
        to_next.start()

    @pl.when(z > 0)
    def _():
        to_prev.start()

    def weight(g, c):
        return wg[g, c * width : (c + 1) * width, :]

    def heads_mix(g, low, high, step=1):
        @pl.loop(0, (high - low) // step)
        def _(i):
            s = low + i * step
            attend(g, s, slot_meta(mol, z, s), mask, qt, kn, vt, probs, share, mixf, mixt, dkt)

    project(z, [weight(z, c) for c in range(3)], nw, SLOT, ROWS, qt, kt, vt, kn, vn, scale)
    heads_mix(z, 1, SLOTS_DEV - 1)
    pick_up(1)

    @pl.when(z > 0)
    def _():
        to_next.wait_recv()

    @pl.when(z == 0)
    def _():
        xh[0] = jnp.zeros_like(xh[0])

    @pl.when(z < last)
    def _():
        to_prev.wait_recv()

    @pl.when(z == last)
    def _():
        xh[1] = jnp.zeros_like(xh[1])

    @pl.loop(0, SLOT // 64)
    def _(i):
        at = pl.multiple_of(i * 64, 64)
        normed(pl.ds(at, 64), xh.at[0], pl.ds(at, 64))
        normed(pl.ds(at + SLOT + ROWS, 64), xh.at[1], pl.ds(at, 64))

    for low in (0, SLOT + ROWS):
        project(z, [None, weight(z, 1), weight(z, 2)], nw, low, SLOT, qt, kt, vt, kn, vn, scale)
    spread[1].step1()
    pick_up(2)
    heads_mix(z, 0, 2 * (SLOTS_DEV - 1), SLOTS_DEV - 1)

    def heads_in(g):
        project(g, [weight(g, c) for c in range(3)], nw, 0, WIN, qt, kt, vt, kn, vn, scale)

    spread[1].step2()
    spread[2].step1()
    pick_up(3)
    spread[1].finish()
    heads_in(near_z[0])
    spread[2].step2()
    spread[3].step1()
    heads_mix(near_z[0], 0, SLOTS_DEV)
    spread[2].finish()
    spread[3].step2()
    heads_in(near_z[1])
    heads_mix(near_z[1], 0, SLOTS_DEV)
    spread[3].finish()
    heads_in(near_z[2])
    heads_mix(near_z[2], 0, SLOTS_DEV)

    mixn = mixt[...].T
    total = x[...].astype(F32)
    for g in range(shards):
        total = total + nn(mixn[:, g * width : (g + 1) * width], weight(g, 3))
    dres[...] = total

    gain_sum[...] = jnp.zeros_like(gain_sum)

    @pl.loop(0, ROWS // 64)
    def _(i):
        at = pl.ds(pl.multiple_of(i * 64, 64), 64)
        zz, _ = norm_stats(dres[at, :])
        nffn[at, :] = (zz * gain_f[...].reshape(1, D)).astype(BF)

    BLK = 256
    for copy in ffn_w:
        copy.wait()

    @pl.loop(0, ROWS // BLK)
    def _(i):
        at = pl.ds(pl.multiple_of(i * BLK, BLK), BLK)
        u = nn(nffn[at, :], wu[...])
        c = cot[at, :]
        dh = nt(c, wd[...])
        cdf = 0.5 + 0.5 * lax.erf(u * SQH)
        h = (u * cdf).astype(BF)
        hidden[at, :] = h
        dinner[at, :] = (dh * (cdf + u * (PHI * jnp.exp(-0.5 * u * u)))).astype(BF)
        out[at, :] = (dres[at, :] + nn(h, wd[...])).astype(BF)

    out_move = move(out, out_to)
    g_ud[1] = tn(hidden[...], cot[...]).astype(BF)
    down = Halve(link, place, g_ud.at[1], *(r.at[shards + 1] for r in (r0, r1, r2, rx)))
    down.start()
    g_ud[0] = tn(nffn[...], dinner[...]).astype(BF)
    up = Halve(link, place, g_ud.at[0], *(r.at[shards] for r in (r0, r1, r2, rx)))
    up.start()
    down.step1()

    @pl.loop(0, ROWS // BLK)
    def _(i):
        at = pl.ds(pl.multiple_of(i * BLK, BLK), BLK)
        dn = nt(dinner[at, :], wu[...])
        zz, r = norm_stats(dres[at, :])
        gain_sum[1:2, :] += jnp.sum(dn * zz, axis=0, keepdims=True)
        dr = cot[at, :].astype(F32) + norm_back(dn, zz, r, gain_f[...].reshape(1, D))
        dres[at, :] = dr
        dbr[at, :] = dr.astype(BF)

    up.step1()
    dkt[...] = jnp.zeros_like(dkt)
    dvt[...] = jnp.zeros_like(dvt)

    def back(g, s):
        attend_back(
            g, s, slot_meta(mol, z, s), mask, qt, kt, vn, dmt, probs, share, mixf, dqkv, dkt, dvt, scale, f_own
        )

    def halo_copy(side, g):
        return pltpu.make_async_remote_copy(
            src_ref=halo_out.at[side, g], dst_ref=halo_in.at[side, g],
            send_sem=halo_send.at[side, g], recv_sem=halo_recv.at[side, g],
            device_id=after if side else before, device_id_type=MESH,
        )

    def border(g):
        dmt[g] = nt(wg[g, 3 * width : 4 * width, :], dbr[...]).astype(BF)

        @pl.loop(0, 2)
        def _(i):
            back(g, i * (SLOTS_DEV - 1))

        for side, cols in ((0, slice(0, SLOT)), (1, slice(SLOT + ROWS, WIN))):
            halo_out[side, g, 0] = dkt[g, :, cols].astype(BF)
            halo_out[side, g, 1] = dvt[g, :, cols].astype(BF)

        @pl.when(z > 0)
        def _():
            halo_copy(0, g).start()

        @pl.when(z < last)
        def _():
            halo_copy(1, g).start()

    def middle(g):
        @pl.loop(1, SLOTS_DEV - 1)
        def _(s):
            back(g, s)

    def shard_grads(k, g):
        @pl.when(z < last)
        def _():
            halo_copy(0, g).wait_recv()
            cols = slice(ROWS, SLOT + ROWS)
            dkt[g, :, cols] += halo_in[0, g, 0].astype(F32)
            dvt[g, :, cols] += halo_in[0, g, 1].astype(F32)

        @pl.when(z > 0)
        def _():
            halo_copy(1, g).wait_recv()
            cols = slice(SLOT, 2 * SLOT)
            dkt[g, :, cols] += halo_in[1, g, 0].astype(F32)
            dvt[g, :, cols] += halo_in[1, g, 1].astype(F32)

        dqkv[g, 1] = dkt[g, :, SLOT : SLOT + ROWS].astype(BF)
        dqkv[g, 2] = dvt[g, :, SLOT : SLOT + ROWS].astype(BF)
        own = nw[SLOT : SLOT + ROWS, :]
        for c in range(3):
            g_k[k, c * width : (c + 1) * width, :] = nn(dqkv[g, c], own).astype(BF)
        at = pl.ds(pl.multiple_of(g * width, 16), width)
        g_k[k, 3 * width : 4 * width, :] = nn(mixt[at, :], dbr[...]).astype(BF)
        job = Halve(link, place, *(r.at[k] for r in (g_k, r0, r1, r2, rx)))
        job.start()
        return job

    def quarter(ref, q):
        lane = q % 2
        c0, ca, cb = place.index(0)
        rows = piece_rows(c0, ca + lane * (cb - ca), cb + lane * (ca - cb), lane)
        return ref.at[rows, pl.ds(pl.multiple_of(q // 2 * (D // 2), 128), D // 2)]

    class Column:
        def __init__(self, i):
            self.g, self.got, self.f, self.spread = g_ud.at[i], zud.at[i], f_ud.at[i], Spread(link, place, f_ud.at[i])

        def send(self):
            self.copies = [
                link.send(quarter(self.g, place.across(k)), self.got.at[k - 1], column(k)) for k in range(1, shards)
            ]

        def sum(self):
            for copy in self.copies:
                copy.wait_recv()
            mine, dst = quarter(self.g, z), quarter(self.f, z)
            add_rows(mine, *[self.got.at[k] for k in range(shards - 1)])
            dst[...] = mine[...]
            self.copies = [link.send(dst, dst, column(k)) for k in range(1, shards)]

        def start(self):
            for copy in self.copies:
                copy.wait_recv()
            self.spread.start()

    up_z, down_z = Column(0), Column(1)
    own_spread = Spread(link, place, f_own)

    def send_shard(k, job):
        return [link.send(job.mine(lane), zk.at[k - 1, lane], column(k)) for lane in range(2)]

    g1, g2, g3 = (place.across(k) for k in (3, 2, 1))
    border(0)
    down.step2()
    border(1)
    up.step2()
    border(2)
    down.step3()
    down_z.send()
    border(3)
    up.step3()
    up_z.send()
    middle(g1)
    down_z.sum()
    job1 = shard_grads(1, g1)
    middle(g2)
    job1.step1()
    up_z.sum()
    job2 = shard_grads(2, g2)
    down_z.start()
    middle(g3)
    job1.step2()
    job2.step1()
    down_z.spread.step1()
    out_move.wait()
    job3 = shard_grads(3, g3)
    up_z.start()
    job1.step3()
    z1 = send_shard(3, job1)
    middle(z)
    job3.step1()
    job2.step2()
    job0 = shard_grads(0, z)
    down_z.spread.step2()
    up_z.spread.step1()

    def tokens_back(low, size):
        at = slice(low, low + size)
        dn = tn(
            dqkv[:, :, :, at].reshape(shards * 3 * width, size),
            jnp.concatenate([wg[g, : 3 * width, :] for g in range(shards)], axis=0),
        )
        zz, r = norm_stats(x[at, :].astype(F32))
        gain_sum[0:1, :] += jnp.sum(dn * zz, axis=0, keepdims=True)
        dres[at, :] = dres[at, :] + norm_back(dn, zz, r, gain_a[...].reshape(1, D))

    tokens_back(0, BLK // 2)
    job0.step1()
    job3.step2()
    job2.step3()
    z2 = send_shard(2, job2)
    tokens_back(BLK // 2, BLK)
    up_z.spread.step2()
    job3.step3()
    z3 = send_shard(1, job3)
    job0.step2()
    tokens_back(BLK // 2 + BLK, BLK // 2)
    move(dres, dtok_to)

    def gain_swap(bit):
        return link.send(gain_sum, gain_got.at[bit], place.near(bit))

    def gain_add(bit, copy):
        copy.wait_recv()
        link.done(copy)
        gain_sum[...] += gain_got[bit]

    swapped = gain_swap(0)
    job0.step3()
    gain_add(0, swapped)
    swapped = gain_swap(1)
    for copy in z1 + z2 + z3:
        copy.wait_recv()
    for lane in range(2):
        mine = job0.mine(lane)
        add_rows(mine, *[zk.at[k, lane] for k in range(shards - 1)])
        f_own.at[piece_rows(*place.index(lane), lane)][...] = mine[...]
    own_spread.start()
    gain_add(1, swapped)
    swapped = gain_swap(2)
    down_z.spread.finish()
    move(f_ud.at[1], down_to)
    own_spread.step1()
    gain_add(2, swapped)
    for bit in range(3, len(place.bits)):
        gain_add(bit, gain_swap(bit))
    gain_col[z] = gain_sum[...]
    gain_copies = [link.send(gain_sum, gain_col.at[z], column(k)) for k in range(1, shards)]
    up_z.spread.finish()
    move(f_ud.at[0], up_to)
    own_spread.step2()
    for copy in gain_copies:
        copy.wait_recv()
    gains_out[...] = sum(gain_col[k] for k in range(shards))
    own_spread.finish()
    move(f_own, own_to)

    link.drain()
    for keep, copies in passed:

        @pl.when(keep)
        def _():
            for copy in copies:
                copy.wait_send()

    @pl.when(z < last)
    def _():
        to_next.wait_send()
        for g in range(shards):
            halo_copy(1, g).wait_send()

    @pl.when(z > 0)
    def _():
        to_prev.wait_send()
        for g in range(shards):
            halo_copy(0, g).wait_send()

    for copy in moves[len(own_w + ffn_w) + 1 :]:
        copy.wait()


VM = pl.BlockSpec(memory_space=pltpu.VMEM)
SM = pl.BlockSpec(memory_space=pltpu.SMEM)
ANY = pl.BlockSpec(memory_space=pl.ANY)
COPIES = 224


def S(shape, dtype):
    return jax.ShapeDtypeStruct(shape, dtype)


def layer(dp_size, n, width, *operands):
    pairs = width // (2 * HEAD_DIM)
    step = 8
    more = 0
    while step < dp_size:
        step *= 2
        more += 1
    extra = max(more, 1)
    bits = 3 + more
    V = pltpu.VMEM
    return pl.pallas_call(
        functools.partial(kernel, dp_size, n),
        out_shape=(
            S((ROWS, D), BF), S((ROWS, D), F32), S((8, D), F32), S((D, D), BF), S((D, D), BF), S((D, D), BF),
        ),
        in_specs=[SM, SM, VM, ANY, VM, VM] + [ANY] * 4,
        out_specs=(ANY, ANY, VM, ANY, ANY, ANY),
        scratch_shapes=[
            V((n, D, D), BF),
            V((ROWS, D), BF),
            V((D, D), BF),
            V((D, D), BF),
            V((2, D, D), BF),
            V((D, D), BF),
            V((WIN, D), BF),
            V((2, SLOT, D), BF),
            V((pairs, width + WIDER, 2 * SLOT), BF),
            V((n, width + WIDER, ROWS), BF),
            V((n, width, WIN), BF),
            V((n, width, WIN), BF),
            V((n, WIN + SLOT, width + WIDER), BF),
            V((n, WIN, width + WIDER), BF),
            V((n, SLOTS_DEV, pairs, 2 * SLOT, 2 * SLOT), BF),
            V((n, width, ROWS), F32),
            V((n, width, ROWS), F32),
            V((D, ROWS), BF),
            V((n, width, ROWS), BF),
            V((ROWS, D), BF),
            V((ROWS, D), F32),
            V((n, 3, width, ROWS), BF),
            V((n, width, WIN), F32),
            V((n, width, WIN), F32),
            V((2, n, 2, width, SLOT), BF),
            V((2, n, 2, width, SLOT), BF),
            V((2, D, D), BF),
            V((n, D, D), BF),
            V((n + 2, D // 2, D), BF),
            V((n + 2, 2, 2, LANE, D), BF),
            V((n + 2, 2, LANE, D), BF),
            V((n + 2, extra, 2, LANE, D), BF),
            V((2, n - 1, LANE, D // 2), BF),
            V((n - 1, 2, LANE, D), BF),
            V((8, D), F32),
            V((bits, 8, D), F32),
            V((n, 8, D), F32),
            pltpu.SemaphoreType.DMA((COPIES + 12 * more,)),
            pltpu.SemaphoreType.DMA((COPIES + 12 * more,)),
            pltpu.SemaphoreType.DMA((2, n)),
            pltpu.SemaphoreType.DMA((2, n)),
            pltpu.SemaphoreType.DMA((16,)),
        ],
        compiler_params=pltpu.CompilerParams(
            vmem_limit_bytes=67043328, collective_id=0, has_side_effects=True
        ),
        name="layer",
    )(*operands)


CHUNK = 128


def finish_kernel(width, out, dtok, gains, up, down, own, *refs):
    outs, (out_v, dtok_v, raw, wide, in_sem, out_sem) = refs[:8], refs[8:]
    out_to, dtok_to, gain_a_to, gain_f_to, qkv_to, wo_to, up_to, down_to = outs
    parts = [(up, up_to, i, i) for i in range(0, D, CHUNK)] + [(down, down_to, i, i) for i in range(0, D, CHUNK)]
    size = CHUNK // 2
    small = [(own, qkv_to, i, i) for i in range(0, 3 * width, size)]
    small += [(own, wo_to, 3 * width + i, i) for i in range(0, width, size)]
    jobs = [(a, b, i, j, CHUNK) for a, b, i, j in parts] + [(a, b, i, j, size) for a, b, i, j in small]
    loads, at = [], 0
    for n, (src, _, i, _, rows) in enumerate(jobs):
        copy = pltpu.make_async_copy(src.at[pl.ds(i, rows)], raw.at[pl.ds(at, rows)], in_sem.at[n])
        copy.start()
        loads.append(copy)
        at += rows
    through = []
    for n, (src, mid, dst) in enumerate(((dtok, dtok_v, dtok_to), (out, out_v, out_to))):
        first = pltpu.make_async_copy(src, mid, in_sem.at[len(jobs) + n])
        first.start()
        through.append((first, pltpu.make_async_copy(mid, dst, out_sem.at[len(jobs) + n])))
    gain_a_to[...] = gains[0, :]
    gain_f_to[...] = gains[1, :]
    stores, at = [], 0
    for n, (_, dst, _, j, rows) in enumerate(jobs):
        loads[n].wait()

        @pl.loop(0, rows // 16)
        def _(i):
            rows16 = pl.ds(pl.multiple_of(at + i * 16, 16), 16)
            wide[rows16, :] = raw[rows16, :].astype(F32)

        copy = pltpu.make_async_copy(wide.at[pl.ds(at, rows)], dst.at[pl.ds(j, rows)], out_sem.at[n])
        copy.start()
        stores.append(copy)
        at += rows
    for first, second in through:
        first.wait()
        second.start()
        stores.append(second)
    for copy in stores:
        copy.wait()


def finish(width, *operands):
    V = pltpu.VMEM
    sems = pltpu.SemaphoreType.DMA((2 * D // CHUNK + 2 * D // CHUNK + 2,))
    return pl.pallas_call(
        functools.partial(finish_kernel, width),
        out_shape=(
            S((ROWS, D), BF), S((ROWS, D), F32), S((D,), F32), S((D,), F32),
            S((3 * width, D), F32), S((width, D), F32), S((D, D), F32), S((D, D), F32),
        ),
        in_specs=[ANY, ANY, VM, ANY, ANY, ANY],
        out_specs=(ANY, ANY, VM, VM, ANY, ANY, ANY, ANY),
        scratch_shapes=[V((ROWS, D), BF), V((ROWS, D), F32), V((3 * D, D), BF), V((3 * D, D), F32), sems, sems],
        name="finish",
    )(*operands)


def local(tokens_in, gain_attn, gain_ffn, w_qkv, w_out, w_up, w_down, slot_mol, slot_fill, cotangent):
    n = lax.axis_size("head")
    width = w_out.shape[0]
    results = layer(
        lax.axis_size("dp"), n, width,
        slot_mol, slot_fill, tokens_in, cotangent, gain_attn, gain_ffn,
        w_qkv.transpose(0, 2, 1).reshape(3 * width, D), w_out, w_up, w_down,
    )
    out, dtok, d_gain_a, d_gain_f, d_qkv, d_wo, d_up, d_down = finish(width, *results)
    return (
        out, dtok, d_gain_a, d_gain_f, d_qkv.reshape(3, width, D).transpose(0, 2, 1), d_wo, d_up, d_down,
    )


def solution(mesh):
    return jax.shard_map(
        local,
        mesh=mesh,
        in_specs=(
            P(("dp", "head"), None), P(), P(), P(None, None, "head"), P("head", None), P(), P(),
            P("dp", None), P("dp", None), P(("dp", "head"), None),
        ),
        out_specs=(
            P(("dp", "head"), None), P(("dp", "head"), None), P(), P(), P(None, None, "head"), P("head", None), P(), P(),
        ),
        check_vma=False,
    )
```

```python
import functools

import jax
import jax.numpy as jnp
from jax import lax
from jax.experimental import pallas as pl
from jax.experimental.pallas import tpu as pltpu
from jax.sharding import PartitionSpec as P

HEAD_DIM = 24
SLOT = 128
D = 768
EPS = 1e-05
SLOTS_DEV = 4
ROWS = SLOTS_DEV * SLOT
WIN = ROWS + 2 * SLOT
BF = jnp.bfloat16
F32 = jnp.float32


def nn(a, b):
    return jnp.dot(a, b, preferred_element_type=F32)


def nt(a, b):
    return lax.dot_general(a, b, (((1,), (1,)), ((), ())), preferred_element_type=F32)


def tn(a, b):
    return lax.dot_general(a, b, (((0,), (0,)), ((), ())), preferred_element_type=F32)


def norm_stats(v):
    mean = jnp.mean(v, axis=-1, keepdims=True)
    centred = v - mean
    var = jnp.mean(centred * centred, axis=-1, keepdims=True)
    r = lax.rsqrt(var + EPS)
    return centred * r, r


def norm_back(grad, z, r, gain):
    e = grad * gain
    return r * (e - jnp.mean(e, -1, keepdims=True) - z * jnp.mean(e * z, -1, keepdims=True))


WIDER = 64


def build_masks(mask_ref, width):
    shape = mask_ref.shape[1:]
    rows = lax.broadcasted_iota(jnp.int32, shape, 0)
    right = (lax.broadcasted_iota(jnp.int32, shape, 1) >= SLOT).astype(jnp.int32)
    for p in range(mask_ref.shape[0]):
        low = (2 * p + right) * HEAD_DIM
        keep = ((rows >= low) & (rows < low + HEAD_DIM)) | (rows >= width)
        mask_ref[p] = jnp.where(keep, 1.0, 0.0).astype(BF)


def extend(fill_ref, z, width, qt, kt, vt, kn, vn):
    lane = lax.broadcasted_iota(jnp.int32, (SLOT, WIDER), 1)
    row = lax.broadcasted_iota(jnp.int32, (SLOT, WIDER), 0)
    ones = jnp.where(lane < 2, 1.0, 0.0).astype(BF)
    top = lax.broadcasted_iota(jnp.int32, (WIDER, ROWS), 0)
    first = jnp.where(top == 0, 1.0, 0.0).astype(BF)
    slots = (WIN + SLOT) // SLOT
    for g in range(qt.shape[0]):
        qt[g, width:, :] = first
        kn[g, WIN:, :width] = jnp.zeros((SLOT, width), BF)
    for s in range(slots):
        live = 0
        if s < slots - 1:
            at = jnp.minimum(jnp.maximum(z * SLOTS_DEV + s - 1, 0), fill_ref.shape[1] - 1)
            live = fill_ref[0, at]
        bias = jnp.where((lane == 0) & (row >= live), -1e30, 0.0).astype(BF)
        for g in range(qt.shape[0]):
            kn[g, s * SLOT : (s + 1) * SLOT, width:] = bias
            if s < slots - 1:
                vn[g, s * SLOT : (s + 1) * SLOT, width:] = ones


def slot_meta(mol_ref, z, s):
    at = z * SLOTS_DEV + s
    last = mol_ref.shape[1] - 1
    before, after = jnp.maximum(at - 1, 0), jnp.minimum(at + 1, last)
    mine = mol_ref[0, at]
    prev = jnp.where((mol_ref[0, before] == mine) & (at > 0), 1, 0)
    nxt = jnp.where((mol_ref[0, after] == mine) & (at < last), 1, 0)
    return prev, nxt * (1 - prev)


def chosen(*terms):
    total = None
    for flag, block in terms:
        term = jnp.broadcast_to(flag.astype(F32), block.shape).astype(BF) * block
        total = term if total is None else total + term
    return total


def pair_rows(full):
    rows = lax.broadcasted_iota(jnp.int32, (2 * HEAD_DIM, SLOT), 0)
    return jnp.where(rows < HEAD_DIM, full[:, :SLOT], full[:, SLOT:])


def project(g, parts, nw, low, count, qt, kt, vt, kn, vn, scale):
    width = kt.shape[1]
    at = slice(low, low + count)
    if parts[0] is not None:
        qt[g, :width, :] = (nt(parts[0], nw[pl.ds(SLOT, ROWS), :]) * scale).astype(BF)
    for part, wide, tall in ((parts[1], kt, kn), (parts[2], vt, vn)):
        rows = nt(part, nw[at, :]).astype(BF)
        wide[g, :, at] = rows
        tall[g, at, :width] = rows.T


def windows(s):
    own = pl.multiple_of((s + 1) * SLOT, SLOT)
    before = pl.multiple_of(s * SLOT, SLOT)
    after = pl.multiple_of((s + 2) * SLOT, SLOT)
    return pl.ds(own, SLOT), pl.ds(before, SLOT), pl.ds(after, SLOT), pl.ds(before, SLOT)


def attend(g, s, meta, mask, qt, kn, vt, probs, share, mixf, mixt, room):
    prev, nxt = meta
    own, before, after, mine = windows(s)
    width = vt.shape[1]
    partner = chosen((prev, kn[g, before, :]), (nxt, kn[g, after, :]), (1 - prev - nxt, kn[g, WIN:, :]))
    keys = jnp.concatenate([kn[g, own, :], partner], axis=0)
    vals = jnp.concatenate([vt[g, :, own], chosen((prev, vt[g, :, before]), (nxt, vt[g, :, after]))], axis=1)
    ones = jnp.ones((16, 2 * SLOT), BF)
    q = qt[g, :, mine]
    q2 = jnp.concatenate([q, q], axis=1)
    pairs = mask.shape[0]
    left, right = slice(0, 2 * SLOT), slice(2 * SLOT, 4 * SLOT)
    tops = [None] * pairs

    def score(p):
        scores = nn(keys, q2 * mask[p])
        room[p, :SLOT, left] = scores[:SLOT]
        room[p, :SLOT, right] = scores[SLOT:]
        tops[p] = jnp.max(scores, axis=0, keepdims=True)

    def weigh(p):
        probs[g, s, p, :SLOT, :] = jnp.exp(room[p, :SLOT, left] - tops[p]).astype(BF)
        probs[g, s, p, SLOT:, :] = jnp.exp(room[p, :SLOT, right] - tops[p]).astype(BF)

    def mix(p):
        head_rows = slice(2 * HEAD_DIM * p, 2 * HEAD_DIM * (p + 1))
        both = nn(jnp.concatenate([vals[head_rows, :], ones], axis=0), probs[g, s, p])
        part = pair_rows(jnp.broadcast_to(1.0 / both[2 * HEAD_DIM : 2 * HEAD_DIM + 1, :], (2 * HEAD_DIM, 2 * SLOT)))
        mixed = pair_rows(both[: 2 * HEAD_DIM, :]) * part
        share[g, head_rows, mine] = part
        mixf[g, head_rows, mine] = mixed
        at = pl.ds(pl.multiple_of(g * width + 2 * HEAD_DIM * p, 16), 2 * HEAD_DIM)
        mixt[at, mine] = mixed.astype(BF)

    for step in range(pairs + 4):
        if step < pairs:
            score(step)
        if 0 <= step - 2 < pairs:
            weigh(step - 2)
        if 0 <= step - 4 < pairs:
            mix(step - 4)


def attend_back(g, s, meta, mask, qt, kt, vn, dmt, probs, share, mixf, dqkv, dkt, dvt, scale, room):
    prev, nxt = meta
    own, before, after, mine = windows(s)
    width = dmt.shape[1]
    fprev, fnext = prev.astype(F32), nxt.astype(F32)
    vals = jnp.concatenate([vn[g, own, :], chosen((prev, vn[g, before, :]), (nxt, vn[g, after, :]))], axis=0)
    keys = jnp.concatenate([kt[g, :, own], chosen((prev, kt[g, :, before]), (nxt, kt[g, :, after]))], axis=1)
    q = qt[g, :width, mine]
    dm = (dmt[g, :, mine].astype(F32) * share[g, :, mine]).astype(BF)
    q2 = jnp.concatenate([q, q], axis=1)
    dm2 = jnp.concatenate([dm, dm], axis=1)
    prod = dm.astype(F32) * mixf[g, :, mine]
    line = lax.broadcasted_iota(jnp.int32, (16, 2 * SLOT), 0)
    rest = jnp.zeros((WIDER - 16, 2 * SLOT), BF)
    pairs = mask.shape[0]
    kept = [None] * pairs

    def rows_of(p):
        return slice(2 * HEAD_DIM * p, 2 * HEAD_DIM * (p + 1))

    def place_of(p):
        return room.at[pl.ds(p // 3 * 2 * SLOT, 2 * SLOT), pl.ds(p % 3 * 2 * SLOT, 2 * SLOT)]

    def slopes(p):
        mid = 2 * HEAD_DIM * p + HEAD_DIM
        inner = jnp.concatenate(
            [
                jnp.sum(prod[2 * HEAD_DIM * p : mid], axis=0, keepdims=True),
                jnp.sum(prod[mid : mid + HEAD_DIM], axis=0, keepdims=True),
            ],
            axis=1,
        )
        high = inner.astype(BF).astype(F32)
        take_off = jnp.where(line == 0, -high, jnp.where(line == 1, high - inner, 0.0)).astype(BF)
        rhs = dm2 * mask[p, :width, :]
        d_probs = nn(vals, jnp.concatenate([rhs, take_off, rest], axis=0))
        place_of(p)[...] = probs[g, s, p] * d_probs.astype(BF)
        kept[p] = nt(rhs[rows_of(p), :], probs[g, s, p])

    def pull(p):
        head_rows = rows_of(p)
        d_scores = place_of(p)[...]
        dq = pair_rows(nn(keys[head_rows, :], d_scores)) * scale
        dqkv[g, 0, head_rows, mine] = dq.astype(BF)
        qm = (q2 * mask[p, :width, :])[head_rows, :]
        dk = nt(qm, d_scores)
        dv = kept[p]
        dkt[g, head_rows, own] += dk[:, :SLOT]
        dvt[g, head_rows, own] += dv[:, :SLOT]
        dkt[g, head_rows, before] += fprev * dk[:, SLOT:]
        dvt[g, head_rows, before] += fprev * dv[:, SLOT:]
        dkt[g, head_rows, after] += fnext * dk[:, SLOT:]
        dvt[g, head_rows, after] += fnext * dv[:, SLOT:]

    for step in range(pairs + 2):
        if step < pairs:
            slopes(step)
        if step >= 2:
            pull(step - 2)


SQH = 0.7071067811865476
PHI = 0.3989422804014327
MESH = pl.DeviceIdType.MESH
HALVINGS = 3
PIECE = D // 8
LANE = PIECE // 2


class Link:
    def __init__(self, send_sem, recv_sem):
        self.send_sem, self.recv_sem, self.used, self.open = send_sem, recv_sem, 0, []

    def reserve(self, count):
        self.used += count
        return self.used - count

    def make(self, src, dst, target, slot=None):
        slot = self.reserve(1) if slot is None else slot
        return pltpu.make_async_remote_copy(
            src_ref=src, dst_ref=dst, send_sem=self.send_sem.at[slot], recv_sem=self.recv_sem.at[slot],
            device_id=target, device_id_type=MESH,
        )

    def send(self, src, dst, target):
        copy = self.make(src, dst, target)
        copy.start()
        self.open.append(copy)
        return copy

    def done(self, copy):
        copy.wait_send()
        self.open = [c for c in self.open if c is not copy]

    def drain(self):
        for copy in self.open:
            copy.wait_send()
        self.open = []


def add_rows(dst, *terms):
    @pl.loop(0, dst.shape[0] // 16)
    def _(i):
        at = pl.ds(pl.multiple_of(i * 16, 16), 16)
        total = dst[at, :].astype(F32)
        for term in terms:
            total = total + term[at, :].astype(F32)
        dst[at, :] = total.astype(dst.dtype)


def piece_rows(d0, d1, d2, lane):
    return pl.ds(pl.multiple_of(((d0 * 2 + d1) * 2 + d2) * PIECE + lane * LANE, 16), LANE)


class Place:
    def __init__(self, dp_size, shards):
        self.dp = lax.axis_index("dp")
        self.z = lax.axis_index("head")
        self.shards = shards
        self.bits, self.partner = [], []
        step = 1
        while step < dp_size:
            bit = (self.dp // step) % 2
            self.bits.append(bit)
            self.partner.append(self.dp + step - 2 * step * bit)
            step *= 2
        self.order = ((0, 1, 2), (0, 2, 1))

    def near(self, bit):
        return {"dp": self.partner[bit]}

    def across(self, k):
        step, found = 1, 0
        while step < self.shards:
            found = found + step * ((self.z // step + k // step) % 2)
            step *= 2
        return found

    def index(self, lane):
        return tuple(self.bits[b] for b in self.order[lane])


class Halve:
    def __init__(self, link, place, g, r0, r1, r2, rx):
        self.link, self.place, self.g, self.r0, self.r1, self.r2, self.rx = link, place, g, r0, r1, r2, rx

    def start(self):
        p = self.place
        self.pass_on, self.keep = [], []
        for side, out in ((1, self.pass_on), (0, self.keep)):
            for lane in range(2):
                c0, c1, _ = p.index(lane)
                d1 = c1 + side * (1 - 2 * c1)
                out.append(
                    [
                        self.link.send(
                            self.g.at[piece_rows(1 - c0, d1, b, lane)], self.r0.at[piece_rows(0, d1, b, lane)], p.near(0)
                        )
                        for b in range(2)
                    ]
                )

    def mine(self, lane):
        return self.g.at[piece_rows(*self.place.index(lane), lane)]

    def step1(self):
        p = self.place
        self.copies = []
        for lane in range(2):
            c0, c1, _ = p.index(lane)
            sent = []
            for b in range(2):
                self.pass_on[lane][b].wait_recv()
                part = self.g.at[piece_rows(c0, 1 - c1, b, lane)]
                add_rows(part, self.r0.at[piece_rows(0, 1 - c1, b, lane)])
                sent.append(self.link.send(part, self.r1.at[lane, b], p.near(p.order[lane][1])))
            self.copies.append(sent)

    def step2(self):
        p = self.place
        old, self.copies = self.copies, []
        for lane in range(2):
            c0, c1, c2 = p.index(lane)
            for b in range(2):
                self.keep[lane][b].wait_recv()
                old[lane][b].wait_recv()
            part = self.g.at[piece_rows(c0, c1, 1 - c2, lane)]
            add_rows(part, self.r0.at[piece_rows(0, c1, 1 - c2, lane)], self.r1.at[lane, 1 - c2])
            self.copies.append(self.link.send(part, self.r2.at[lane], p.near(p.order[lane][2])))

    def step3(self):
        p = self.place
        for lane in range(2):
            _, c1, c2 = p.index(lane)
            self.copies[lane].wait_recv()
            add_rows(self.mine(lane), self.r0.at[piece_rows(0, c1, c2, lane)], self.r1.at[lane, c2], self.r2.at[lane])
        for extra in range(HALVINGS, len(p.bits)):
            copies = [
                self.link.send(self.mine(lane), self.rx.at[extra - HALVINGS, lane], p.near(extra)) for lane in range(2)
            ]
            for lane in range(2):
                copies[lane].wait_recv()
                self.link.done(copies[lane])
                add_rows(self.mine(lane), self.rx.at[extra - HALVINGS, lane])


class Spread:
    def __init__(self, link, place, f):
        self.link, self.place, self.f = link, place, f

    def swap(self, rows, bit):
        part = self.f.at[rows]
        return self.link.send(part, part, self.place.near(bit))

    def begin(self):
        self.first, self.second, self.core = [], [[], []], []

    def pass_on(self, lane, rows):
        self.second[lane].append(self.swap(rows, self.place.order[lane][1]))
        self.core.append(self.swap(rows, 0))

    def start(self):
        p = self.place
        self.begin()
        for lane in range(2):
            own = piece_rows(*p.index(lane), lane)
            self.first.append(self.swap(own, p.order[lane][2]))
            self.pass_on(lane, own)

    def step1(self):
        p = self.place
        for lane in range(2):
            c0, c1, c2 = p.index(lane)
            self.first[lane].wait_recv()
            self.pass_on(lane, piece_rows(c0, c1, 1 - c2, lane))

    def step2(self):
        p = self.place
        for lane in range(2):
            c0, c1, c2 = p.index(lane)
            for copy in self.second[lane]:
                copy.wait_recv()
            for b in range(2):
                self.core.append(self.swap(piece_rows(c0, 1 - c1, b, lane), 0))

    def finish(self):
        for copy in self.core:
            copy.wait_recv()


def kernel(
    dp_size, shards,
    mol, fill, x, cot_in, gain_a, gain_f, qkv_in, wo_in, wu_in, wd_in,
    out_to, dtok_to, gains_out, up_to, down_to, own_to,
    wg, cot, wu, wd, f_ud, f_own,
    nw, xh, mask, qt, kt, vt, kn, vn, probs, share, mixf, mixt, dmt, dbr, dres,
    dqkv, dkt, dvt, halo_out, halo_in, g_ud, g_k, r0, r1, r2, rx, zud, zk,
    gain_sum, gain_got, gain_col,
    send_sem, recv_sem, halo_send, halo_recv, load_sem,
):
    place = Place(dp_size, shards)
    link = Link(send_sem, recv_sem)
    z = place.z
    last = shards - 1
    nffn, hidden, dinner, out = (g_k.at[i, pl.ds(0, ROWS)] for i in range(4))
    scale = HEAD_DIM ** (-0.5)
    width = dmt.shape[1]

    def column(k):
        return {"head": place.across(k)}

    moves = []

    def move(src, dst):
        copy = pltpu.make_async_copy(src, dst, load_sem.at[len(moves)])
        copy.start()
        moves.append(copy)
        return copy

    own_w = [
        move(qkv_in, wg.at[z, pl.ds(0, 3 * width)]),
        move(wo_in, wg.at[z, pl.ds(3 * width, width)]),
    ]
    ffn_w = [move(wu_in, wu), move(wd_in, wd), move(cot_in, cot)]

    barrier = pltpu.get_barrier_semaphore()
    peers = [place.near(b) for b in range(len(place.bits))] + [column(k) for k in range(1, shards)]
    for peer in peers:
        pl.semaphore_signal(barrier, inc=1, device_id=peer, device_id_type=MESH)
    pl.semaphore_wait(barrier, len(peers))

    after = {"head": jnp.minimum(z + 1, last)}
    before = {"head": jnp.maximum(z - 1, 0)}
    to_next = link.make(x.at[pl.ds(ROWS - SLOT, SLOT)], xh.at[0], after)
    to_prev = link.make(x.at[pl.ds(0, SLOT)], xh.at[1], before)

    for copy in own_w:
        copy.wait()
    lanes = [piece_rows(*place.index(lane), lane) for lane in range(2)]
    inner = (z > 0) & (z < last)
    outer = (z == 0) | (z == last)
    near_z = [place.across(1), 2 - z // 2, last - last * (z // 2)]
    line = link.reserve(max(10, 2 * shards))
    passed = []

    def along(g, target, step):
        return [
            pltpu.make_async_remote_copy(
                src_ref=wg.at[g, rows], dst_ref=wg.at[g, rows],
                send_sem=send_sem.at[line + 2 * step + lane], recv_sem=recv_sem.at[line + 2 * g + lane],
                device_id={"head": target}, device_id_type=MESH,
            )
            for lane, rows in enumerate(lanes)
        ]

    def pass_on(keep, g, target, step):
        copies = along(g, target, step)
        passed.append((keep, copies))

        @pl.when(keep)
        def _():
            for copy in copies:
                copy.start()

    def arrived(g):
        for copy in along(g, after["head"], 0):
            copy.wait_recv()

    pass_on(z < last, z, after["head"], 0)
    pass_on(z > 0, z, before["head"], 1)
    spread = [None] + [Spread(link, place, wg.at[g]) for g in near_z]

    def pick_up(step):
        first, second, third = near_z
        if step == 1:
            arrived(first)
            pass_on(inner, first, last - z, 2)

            @pl.when(inner)
            def _():
                arrived(second)

            pass_on(inner, second, last * (z // 2), 3)
        if step == 2:

            @pl.when(outer)
            def _():
                arrived(second)

            @pl.when(inner)
            def _():
                arrived(third)

            pass_on(inner, third, last * (z // 2), 4)
        if step == 3:

            @pl.when(outer)
            def _():
                arrived(third)

        spread[step].start()

    build_masks(mask, width)
    extend(fill, z, width, qt, kt, vt, kn, vn)

    def normed(at_w, ref, at):
        zz, _ = norm_stats(ref[at, :].astype(F32))
        nw[at_w, :] = (zz * gain_a[...].reshape(1, D)).astype(BF)

    @pl.loop(0, ROWS // 64)
    def _(i):
        at = pl.multiple_of(i * 64, 64)
        normed(pl.ds(at + SLOT, 64), x, pl.ds(at, 64))

    @pl.when(z < last)
    def _():
        to_next.start()

    @pl.when(z > 0)
    def _():
        to_prev.start()

    def weight(g, c):
        return wg[g, c * width : (c + 1) * width, :]

    def heads_mix(g, low, high, step=1):
        @pl.loop(0, (high - low) // step)
        def _(i):
            s = low + i * step
            attend(g, s, slot_meta(mol, z, s), mask, qt, kn, vt, probs, share, mixf, mixt, dkt)

    project(z, [weight(z, c) for c in range(3)], nw, SLOT, ROWS, qt, kt, vt, kn, vn, scale)
    pick_up(1)
    heads_mix(z, 1, SLOTS_DEV - 1)
    spread[1].step1()

    @pl.when(z > 0)
    def _():
        to_next.wait_recv()

    @pl.when(z == 0)
    def _():
        xh[0] = jnp.zeros_like(xh[0])

    @pl.when(z < last)
    def _():
        to_prev.wait_recv()

    @pl.when(z == last)
    def _():
        xh[1] = jnp.zeros_like(xh[1])

    @pl.loop(0, SLOT // 64)
    def _(i):
        at = pl.multiple_of(i * 64, 64)
        normed(pl.ds(at, 64), xh.at[0], pl.ds(at, 64))
        normed(pl.ds(at + SLOT + ROWS, 64), xh.at[1], pl.ds(at, 64))

    for low in (0, SLOT + ROWS):
        project(z, [None, weight(z, 1), weight(z, 2)], nw, low, SLOT, qt, kt, vt, kn, vn, scale)
    pick_up(2)
    spread[1].step2()
    heads_mix(z, 0, 2 * (SLOTS_DEV - 1), SLOTS_DEV - 1)

    def mix_out(g):
        at = pl.ds(pl.multiple_of(g * width, 16), width)
        dres[...] += tn(mixt[at, :], weight(g, 3))

    def heads_in(g):
        project(g, [weight(g, c) for c in range(3)], nw, 0, WIN, qt, kt, vt, kn, vn, scale)

    spread[2].step1()
    pick_up(3)
    dres[...] = x[...].astype(F32)
    mix_out(z)
    for copy in ffn_w:
        copy.wait()
    for i in range(ROWS // SLOT):
        dvt[i, :SLOT, :] = nt(cot[i * SLOT : (i + 1) * SLOT, :], wd[...])
    spread[1].finish()
    heads_in(near_z[0])
    spread[2].step2()
    spread[3].step1()
    heads_mix(near_z[0], 0, SLOTS_DEV)
    mix_out(near_z[0])
    spread[2].finish()
    spread[3].step2()
    heads_in(near_z[1])
    heads_mix(near_z[1], 0, SLOTS_DEV)
    mix_out(near_z[1])
    spread[3].finish()
    heads_in(near_z[2])
    heads_mix(near_z[2], 0, SLOTS_DEV)
    mix_out(near_z[2])

    gain_sum[...] = jnp.zeros_like(gain_sum)
    BLK = 256

    @pl.loop(0, ROWS // BLK)
    def _(i):
        at = pl.ds(pl.multiple_of(i * BLK, BLK), BLK)
        zz, _ = norm_stats(dres[at, :])
        normed_ffn = (zz * gain_f[...].reshape(1, D)).astype(BF)
        nffn[at, :] = normed_ffn
        u = nn(normed_ffn, wu[...])
        dh = jnp.concatenate([dvt[2 * i, :SLOT, :], dvt[2 * i + 1, :SLOT, :]], axis=0)
        cdf = 0.5 + 0.5 * lax.erf(u * SQH)
        h = (u * cdf).astype(BF)
        hidden[at, :] = h
        dinner[at, :] = (dh * (cdf + u * (PHI * jnp.exp(-0.5 * u * u)))).astype(BF)
        out[at, :] = (dres[at, :] + nn(h, wd[...])).astype(BF)

    out_move = move(out, out_to)
    dkt[...] = jnp.zeros_like(dkt)
    dvt[...] = jnp.zeros_like(dvt)
    g_ud[1] = tn(hidden[...], cot[...]).astype(BF)
    down = Halve(link, place, g_ud.at[1], *(r.at[shards + 1] for r in (r0, r1, r2, rx)))
    down.start()
    g_ud[0] = tn(nffn[...], dinner[...]).astype(BF)
    up = Halve(link, place, g_ud.at[0], *(r.at[shards] for r in (r0, r1, r2, rx)))
    up.start()
    down.step1()

    @pl.loop(0, ROWS // BLK)
    def _(i):
        at = pl.ds(pl.multiple_of(i * BLK, BLK), BLK)
        dn = nt(dinner[at, :], wu[...])
        zz, r = norm_stats(dres[at, :])
        gain_sum[1:2, :] += jnp.sum(dn * zz, axis=0, keepdims=True)
        dr = cot[at, :].astype(F32) + norm_back(dn, zz, r, gain_f[...].reshape(1, D))
        dres[at, :] = dr
        dbr[at, :] = dr.astype(BF)

    up.step1()

    def back(g, s):
        attend_back(
            g, s, slot_meta(mol, z, s), mask, qt, kt, vn, dmt, probs, share, mixf, dqkv, dkt, dvt, scale, f_own
        )

    def halo_copy(side, g):
        return pltpu.make_async_remote_copy(
            src_ref=halo_out.at[side, g], dst_ref=halo_in.at[side, g],
            send_sem=halo_send.at[side, g], recv_sem=halo_recv.at[side, g],
            device_id=after if side else before, device_id_type=MESH,
        )

    def border(g):
        dmt[g] = nt(wg[g, 3 * width : 4 * width, :], dbr[...]).astype(BF)

        @pl.loop(0, 2)
        def _(i):
            back(g, i * (SLOTS_DEV - 1))

        for side, cols in ((0, slice(0, SLOT)), (1, slice(SLOT + ROWS, WIN))):
            halo_out[side, g, 0] = dkt[g, :, cols].astype(BF)
            halo_out[side, g, 1] = dvt[g, :, cols].astype(BF)

        @pl.when(z > 0)
        def _():
            halo_copy(0, g).start()

        @pl.when(z < last)
        def _():
            halo_copy(1, g).start()

    def middle(g):
        @pl.loop(1, SLOTS_DEV - 1)
        def _(s):
            back(g, s)

    def shard_grads(k, g):
        @pl.when(z < last)
        def _():
            halo_copy(0, g).wait_recv()
            cols = slice(ROWS, SLOT + ROWS)
            dkt[g, :, cols] += halo_in[0, g, 0].astype(F32)
            dvt[g, :, cols] += halo_in[0, g, 1].astype(F32)

        @pl.when(z > 0)
        def _():
            halo_copy(1, g).wait_recv()
            cols = slice(SLOT, 2 * SLOT)
            dkt[g, :, cols] += halo_in[1, g, 0].astype(F32)
            dvt[g, :, cols] += halo_in[1, g, 1].astype(F32)

        dqkv[g, 1] = dkt[g, :, SLOT : SLOT + ROWS].astype(BF)
        dqkv[g, 2] = dvt[g, :, SLOT : SLOT + ROWS].astype(BF)
        own = nw[SLOT : SLOT + ROWS, :]
        for c in range(3):
            g_k[k, c * width : (c + 1) * width, :] = nn(dqkv[g, c], own).astype(BF)
        at = pl.ds(pl.multiple_of(g * width, 16), width)
        g_k[k, 3 * width : 4 * width, :] = nn(mixt[at, :], dbr[...]).astype(BF)
        job = Halve(link, place, *(r.at[k] for r in (g_k, r0, r1, r2, rx)))
        job.start()
        return job

    def quarter(ref, q):
        lane = q % 2
        c0, ca, cb = place.index(0)
        rows = piece_rows(c0, ca + lane * (cb - ca), cb + lane * (ca - cb), lane)
        return ref.at[rows, pl.ds(pl.multiple_of(q // 2 * (D // 2), 128), D // 2)]

    class Column:
        def __init__(self, i):
            self.g, self.got, self.f, self.spread = g_ud.at[i], zud.at[i], f_ud.at[i], Spread(link, place, f_ud.at[i])

        def send(self):
            self.copies = [
                link.send(quarter(self.g, place.across(k)), self.got.at[k - 1], column(k)) for k in range(1, shards)
            ]

        def sum(self):
            for copy in self.copies:
                copy.wait_recv()
            mine, dst = quarter(self.g, z), quarter(self.f, z)
            add_rows(mine, *[self.got.at[k] for k in range(shards - 1)])
            dst[...] = mine[...]
            self.copies = [link.send(dst, dst, column(k)) for k in range(1, shards)]

        def start(self):
            for copy in self.copies:
                copy.wait_recv()
            self.spread.start()

    up_z, down_z = Column(0), Column(1)
    own_spread = Spread(link, place, f_own)

    def send_shard(k, job):
        return [link.send(job.mine(lane), zk.at[k - 1, lane], column(k)) for lane in range(2)]

    g1, g2, g3 = (place.across(k) for k in (3, 2, 1))
    border(0)
    down.step2()
    border(1)
    up.step2()
    border(2)
    down.step3()
    down_z.send()
    border(3)
    up.step3()
    up_z.send()
    middle(g1)
    down_z.sum()
    job1 = shard_grads(1, g1)
    middle(g2)
    job1.step1()
    up_z.sum()
    job2 = shard_grads(2, g2)
    down_z.start()
    middle(g3)
    job1.step2()
    job2.step1()
    down_z.spread.step1()
    out_move.wait()
    job3 = shard_grads(3, g3)
    up_z.start()
    job1.step3()
    z1 = send_shard(3, job1)
    middle(z)
    job3.step1()
    job2.step2()
    job0 = shard_grads(0, z)
    down_z.spread.step2()
    up_z.spread.step1()

    def tokens_back(low, size):
        at = slice(low, low + size)
        dn = tn(
            dqkv[:, :, :, at].reshape(shards * 3 * width, size),
            jnp.concatenate([wg[g, : 3 * width, :] for g in range(shards)], axis=0),
        )
        zz, r = norm_stats(x[at, :].astype(F32))
        gain_sum[0:1, :] += jnp.sum(dn * zz, axis=0, keepdims=True)
        dres[at, :] = dres[at, :] + norm_back(dn, zz, r, gain_a[...].reshape(1, D))

    tokens_back(0, BLK // 2)
    job0.step1()
    job3.step2()
    job2.step3()
    z2 = send_shard(2, job2)
    tokens_back(BLK // 2, BLK)
    up_z.spread.step2()
    job3.step3()
    z3 = send_shard(1, job3)
    job0.step2()
    tokens_back(BLK // 2 + BLK, BLK // 2)
    move(dres, dtok_to)

    def gain_swap(bit):
        return link.send(gain_sum, gain_got.at[bit], place.near(bit))

    def gain_add(bit, copy):
        copy.wait_recv()
        link.done(copy)
        gain_sum[...] += gain_got[bit]

    swapped = gain_swap(0)
    job0.step3()
    gain_add(0, swapped)
    swapped = gain_swap(1)
    for copy in z1 + z2 + z3:
        copy.wait_recv()
    for lane in range(2):
        mine = job0.mine(lane)
        add_rows(mine, *[zk.at[k, lane] for k in range(shards - 1)])
        f_own.at[piece_rows(*place.index(lane), lane)][...] = mine[...]
    own_spread.start()
    gain_add(1, swapped)
    swapped = gain_swap(2)
    down_z.spread.finish()
    move(f_ud.at[1], down_to)
    own_spread.step1()
    gain_add(2, swapped)
    for bit in range(3, len(place.bits)):
        gain_add(bit, gain_swap(bit))
    gain_col[z] = gain_sum[...]
    gain_copies = [link.send(gain_sum, gain_col.at[z], column(k)) for k in range(1, shards)]
    up_z.spread.finish()
    move(f_ud.at[0], up_to)
    own_spread.step2()
    for copy in gain_copies:
        copy.wait_recv()
    gains_out[...] = sum(gain_col[k] for k in range(shards))
    own_spread.finish()
    move(f_own, own_to)

    link.drain()
    for keep, copies in passed:

        @pl.when(keep)
        def _():
            for copy in copies:
                copy.wait_send()

    @pl.when(z < last)
    def _():
        to_next.wait_send()
        for g in range(shards):
            halo_copy(1, g).wait_send()

    @pl.when(z > 0)
    def _():
        to_prev.wait_send()
        for g in range(shards):
            halo_copy(0, g).wait_send()

    for copy in moves[len(own_w + ffn_w) + 1 :]:
        copy.wait()


VM = pl.BlockSpec(memory_space=pltpu.VMEM)
SM = pl.BlockSpec(memory_space=pltpu.SMEM)
ANY = pl.BlockSpec(memory_space=pl.ANY)
COPIES = 224


def S(shape, dtype):
    return jax.ShapeDtypeStruct(shape, dtype)


def layer(dp_size, n, width, *operands):
    pairs = width // (2 * HEAD_DIM)
    step = 8
    more = 0
    while step < dp_size:
        step *= 2
        more += 1
    extra = max(more, 1)
    bits = 3 + more
    V = pltpu.VMEM
    return pl.pallas_call(
        functools.partial(kernel, dp_size, n),
        out_shape=(
            S((ROWS, D), BF), S((ROWS, D), F32), S((8, D), F32), S((D, D), BF), S((D, D), BF), S((D, D), BF),
        ),
        in_specs=[SM, SM, VM, ANY, VM, VM] + [ANY] * 4,
        out_specs=(ANY, ANY, VM, ANY, ANY, ANY),
        scratch_shapes=[
            V((n, D, D), BF),
            V((ROWS, D), BF),
            V((D, D), BF),
            V((D, D), BF),
            V((2, D, D), BF),
            V((D, D), BF),
            V((WIN, D), BF),
            V((2, SLOT, D), BF),
            V((pairs, width + WIDER, 2 * SLOT), BF),
            V((n, width + WIDER, ROWS), BF),
            V((n, width, WIN), BF),
            V((n, width, WIN), BF),
            V((n, WIN + SLOT, width + WIDER), BF),
            V((n, WIN, width + WIDER), BF),
            V((n, SLOTS_DEV, pairs, 2 * SLOT, 2 * SLOT), BF),
            V((n, width, ROWS), F32),
            V((n, width, ROWS), F32),
            V((D, ROWS), BF),
            V((n, width, ROWS), BF),
            V((ROWS, D), BF),
            V((ROWS, D), F32),
            V((n, 3, width, ROWS), BF),
            V((n, width, WIN), F32),
            V((n, width, WIN), F32),
            V((2, n, 2, width, SLOT), BF),
            V((2, n, 2, width, SLOT), BF),
            V((2, D, D), BF),
            V((n, D, D), BF),
            V((n + 2, D // 2, D), BF),
            V((n + 2, 2, 2, LANE, D), BF),
            V((n + 2, 2, LANE, D), BF),
            V((n + 2, extra, 2, LANE, D), BF),
            V((2, n - 1, LANE, D // 2), BF),
            V((n - 1, 2, LANE, D), BF),
            V((8, D), F32),
            V((bits, 8, D), F32),
            V((n, 8, D), F32),
            pltpu.SemaphoreType.DMA((COPIES + 12 * more,)),
            pltpu.SemaphoreType.DMA((COPIES + 12 * more,)),
            pltpu.SemaphoreType.DMA((2, n)),
            pltpu.SemaphoreType.DMA((2, n)),
            pltpu.SemaphoreType.DMA((16,)),
        ],
        compiler_params=pltpu.CompilerParams(
            vmem_limit_bytes=67043328, collective_id=0, has_side_effects=True
        ),
        name="layer",
    )(*operands)


CHUNK = 128


def finish_kernel(width, out, dtok, gains, up, down, own, *refs):
    outs, (out_v, dtok_v, raw, wide, in_sem, out_sem) = refs[:8], refs[8:]
    out_to, dtok_to, gain_a_to, gain_f_to, qkv_to, wo_to, up_to, down_to = outs
    parts = [(up, up_to, i, i) for i in range(0, D, CHUNK)] + [(down, down_to, i, i) for i in range(0, D, CHUNK)]
    size = CHUNK // 2
    small = [(own, qkv_to, i, i) for i in range(0, 3 * width, size)]
    small += [(own, wo_to, 3 * width + i, i) for i in range(0, width, size)]
    jobs = [(a, b, i, j, CHUNK) for a, b, i, j in parts] + [(a, b, i, j, size) for a, b, i, j in small]
    loads, at = [], 0
    for n, (src, _, i, _, rows) in enumerate(jobs):
        copy = pltpu.make_async_copy(src.at[pl.ds(i, rows)], raw.at[pl.ds(at, rows)], in_sem.at[n])
        copy.start()
        loads.append(copy)
        at += rows
    through = []
    for n, (src, mid, dst) in enumerate(((dtok, dtok_v, dtok_to), (out, out_v, out_to))):
        first = pltpu.make_async_copy(src, mid, in_sem.at[len(jobs) + n])
        first.start()
        through.append((first, pltpu.make_async_copy(mid, dst, out_sem.at[len(jobs) + n])))
    gain_a_to[...] = gains[0, :]
    gain_f_to[...] = gains[1, :]
    stores, at = [], 0
    for n, (_, dst, _, j, rows) in enumerate(jobs):
        loads[n].wait()

        @pl.loop(0, rows // 16)
        def _(i):
            rows16 = pl.ds(pl.multiple_of(at + i * 16, 16), 16)
            wide[rows16, :] = raw[rows16, :].astype(F32)

        copy = pltpu.make_async_copy(wide.at[pl.ds(at, rows)], dst.at[pl.ds(j, rows)], out_sem.at[n])
        copy.start()
        stores.append(copy)
        at += rows
    for first, second in through:
        first.wait()
        second.start()
        stores.append(second)
    for copy in stores:
        copy.wait()


def finish(width, *operands):
    V = pltpu.VMEM
    sems = pltpu.SemaphoreType.DMA((2 * D // CHUNK + 2 * D // CHUNK + 2,))
    return pl.pallas_call(
        functools.partial(finish_kernel, width),
        out_shape=(
            S((ROWS, D), BF), S((ROWS, D), F32), S((D,), F32), S((D,), F32),
            S((3 * width, D), F32), S((width, D), F32), S((D, D), F32), S((D, D), F32),
        ),
        in_specs=[ANY, ANY, VM, ANY, ANY, ANY],
        out_specs=(ANY, ANY, VM, VM, ANY, ANY, ANY, ANY),
        scratch_shapes=[V((ROWS, D), BF), V((ROWS, D), F32), V((3 * D, D), BF), V((3 * D, D), F32), sems, sems],
        name="finish",
    )(*operands)


def local(tokens_in, gain_attn, gain_ffn, w_qkv, w_out, w_up, w_down, slot_mol, slot_fill, cotangent):
    n = lax.axis_size("head")
    width = w_out.shape[0]
    results = layer(
        lax.axis_size("dp"), n, width,
        slot_mol, slot_fill, tokens_in, cotangent, gain_attn, gain_ffn,
        w_qkv.transpose(0, 2, 1).reshape(3 * width, D), w_out, w_up, w_down,
    )
    out, dtok, d_gain_a, d_gain_f, d_qkv, d_wo, d_up, d_down = finish(width, *results)
    return (
        out, dtok, d_gain_a, d_gain_f, d_qkv.reshape(3, width, D).transpose(0, 2, 1), d_wo, d_up, d_down,
    )


def solution(mesh):
    return jax.shard_map(
        local,
        mesh=mesh,
        in_specs=(
            P(("dp", "head"), None), P(), P(), P(None, None, "head"), P("head", None), P(), P(),
            P("dp", None), P("dp", None), P(("dp", "head"), None),
        ),
        out_specs=(
            P(("dp", "head"), None), P(("dp", "head"), None), P(), P(), P(None, None, "head"), P("head", None), P(), P(),
        ),
        check_vma=False,
    )
```

```python
import functools

import jax
import jax.numpy as jnp
from jax import lax
from jax.experimental import pallas as pl
from jax.experimental.pallas import tpu as pltpu
from jax.sharding import PartitionSpec as P

HEAD_DIM = 24
SLOT = 128
D = 768
EPS = 1e-05
SLOTS_DEV = 4
ROWS = SLOTS_DEV * SLOT
WIN = ROWS + 2 * SLOT
BF = jnp.bfloat16
F32 = jnp.float32


def nn(a, b):
    return jnp.dot(a, b, preferred_element_type=F32)


def nt(a, b):
    return lax.dot_general(a, b, (((1,), (1,)), ((), ())), preferred_element_type=F32)


def tn(a, b):
    return lax.dot_general(a, b, (((0,), (0,)), ((), ())), preferred_element_type=F32)


def norm_stats(v):
    mean = jnp.mean(v, axis=-1, keepdims=True)
    centred = v - mean
    var = jnp.mean(centred * centred, axis=-1, keepdims=True)
    r = lax.rsqrt(var + EPS)
    return centred * r, r


def norm_back(grad, z, r, gain):
    e = grad * gain
    return r * (e - jnp.mean(e, -1, keepdims=True) - z * jnp.mean(e * z, -1, keepdims=True))


WIDER = 64


def build_masks(mask_ref, width):
    shape = mask_ref.shape[1:]
    rows = lax.broadcasted_iota(jnp.int32, shape, 0)
    right = (lax.broadcasted_iota(jnp.int32, shape, 1) >= SLOT).astype(jnp.int32)
    for p in range(mask_ref.shape[0]):
        low = (2 * p + right) * HEAD_DIM
        keep = ((rows >= low) & (rows < low + HEAD_DIM)) | (rows >= width)
        mask_ref[p] = jnp.where(keep, 1.0, 0.0).astype(BF)


def extend(fill_ref, z, width, qt, kt, vt, kn, vn):
    lane = lax.broadcasted_iota(jnp.int32, (SLOT, WIDER), 1)
    row = lax.broadcasted_iota(jnp.int32, (SLOT, WIDER), 0)
    ones = jnp.where(lane < 2, 1.0, 0.0).astype(BF)
    top = lax.broadcasted_iota(jnp.int32, (WIDER, ROWS), 0)
    first = jnp.where(top == 0, 1.0, 0.0).astype(BF)
    slots = (WIN + SLOT) // SLOT
    for g in range(qt.shape[0]):
        qt[g, width:, :] = first
        kn[g, WIN:, :width] = jnp.zeros((SLOT, width), BF)
    for s in range(slots):
        live = 0
        if s < slots - 1:
            at = jnp.minimum(jnp.maximum(z * SLOTS_DEV + s - 1, 0), fill_ref.shape[1] - 1)
            live = fill_ref[0, at]
        bias = jnp.where((lane == 0) & (row >= live), -1e30, 0.0).astype(BF)
        for g in range(qt.shape[0]):
            kn[g, s * SLOT : (s + 1) * SLOT, width:] = bias
            if s < slots - 1:
                vn[g, s * SLOT : (s + 1) * SLOT, width:] = ones


def slot_meta(mol_ref, z, s):
    at = z * SLOTS_DEV + s
    last = mol_ref.shape[1] - 1
    before, after = jnp.maximum(at - 1, 0), jnp.minimum(at + 1, last)
    mine = mol_ref[0, at]
    prev = jnp.where((mol_ref[0, before] == mine) & (at > 0), 1, 0)
    nxt = jnp.where((mol_ref[0, after] == mine) & (at < last), 1, 0)
    return prev, nxt * (1 - prev)


def chosen(*terms):
    total = None
    for flag, block in terms:
        term = jnp.broadcast_to(flag.astype(F32), block.shape).astype(BF) * block
        total = term if total is None else total + term
    return total


def pair_rows(full):
    rows = lax.broadcasted_iota(jnp.int32, (2 * HEAD_DIM, SLOT), 0)
    return jnp.where(rows < HEAD_DIM, full[:, :SLOT], full[:, SLOT:])


def project(g, parts, nw, low, count, qt, kt, vt, kn, vn, scale):
    width = kt.shape[1]
    at = slice(low, low + count)
    if parts[0] is not None:
        qt[g, :width, :] = (nt(parts[0], nw[pl.ds(SLOT, ROWS), :]) * scale).astype(BF)
    for part, wide, tall in ((parts[1], kt, kn), (parts[2], vt, vn)):
        rows = nt(part, nw[at, :]).astype(BF)
        wide[g, :, at] = rows
        tall[g, at, :width] = rows.T


def windows(s):
    own = pl.multiple_of((s + 1) * SLOT, SLOT)
    before = pl.multiple_of(s * SLOT, SLOT)
    after = pl.multiple_of((s + 2) * SLOT, SLOT)
    return pl.ds(own, SLOT), pl.ds(before, SLOT), pl.ds(after, SLOT), pl.ds(before, SLOT)


def attend(g, s, meta, mask, qt, kn, vt, probs, share, mixf, mixt, room):
    prev, nxt = meta
    own, before, after, mine = windows(s)
    width = vt.shape[1]
    partner = chosen((prev, kn[g, before, :]), (nxt, kn[g, after, :]), (1 - prev - nxt, kn[g, WIN:, :]))
    keys = jnp.concatenate([kn[g, own, :], partner], axis=0)
    vals = jnp.concatenate([vt[g, :, own], chosen((prev, vt[g, :, before]), (nxt, vt[g, :, after]))], axis=1)
    ones = jnp.ones((16, 2 * SLOT), BF)
    q = qt[g, :, mine]
    q2 = jnp.concatenate([q, q], axis=1)
    pairs = mask.shape[0]
    left, right = slice(0, 2 * SLOT), slice(2 * SLOT, 4 * SLOT)
    tops = [None] * pairs

    def score(p):
        scores = nn(keys, q2 * mask[p])
        room[p, :SLOT, left] = scores[:SLOT]
        room[p, :SLOT, right] = scores[SLOT:]
        tops[p] = jnp.max(scores, axis=0, keepdims=True)

    def weigh(p):
        probs[g, s, p, :SLOT, :] = jnp.exp(room[p, :SLOT, left] - tops[p]).astype(BF)
        probs[g, s, p, SLOT:, :] = jnp.exp(room[p, :SLOT, right] - tops[p]).astype(BF)

    def mix(p):
        head_rows = slice(2 * HEAD_DIM * p, 2 * HEAD_DIM * (p + 1))
        both = nn(jnp.concatenate([vals[head_rows, :], ones], axis=0), probs[g, s, p])
        part = pair_rows(jnp.broadcast_to(1.0 / both[2 * HEAD_DIM : 2 * HEAD_DIM + 1, :], (2 * HEAD_DIM, 2 * SLOT)))
        mixed = pair_rows(both[: 2 * HEAD_DIM, :]) * part
        share[g, head_rows, mine] = part
        mixf[g, head_rows, mine] = mixed
        at = pl.ds(pl.multiple_of(g * width + 2 * HEAD_DIM * p, 16), 2 * HEAD_DIM)
        mixt[at, mine] = mixed.astype(BF)

    for step in range(pairs + 4):
        if step < pairs:
            score(step)
        if 0 <= step - 2 < pairs:
            weigh(step - 2)
        if 0 <= step - 4 < pairs:
            mix(step - 4)


def attend_back(g, s, meta, mask, qt, kt, vn, dmt, probs, share, mixf, dqkv, dkt, dvt, scale, room):
    prev, nxt = meta
    own, before, after, mine = windows(s)
    width = dmt.shape[1]
    fprev, fnext = prev.astype(F32), nxt.astype(F32)
    vals = jnp.concatenate([vn[g, own, :], chosen((prev, vn[g, before, :]), (nxt, vn[g, after, :]))], axis=0)
    keys = jnp.concatenate([kt[g, :, own], chosen((prev, kt[g, :, before]), (nxt, kt[g, :, after]))], axis=1)
    q = qt[g, :width, mine]
    dm = (dmt[g, :, mine].astype(F32) * share[g, :, mine]).astype(BF)
    q2 = jnp.concatenate([q, q], axis=1)
    dm2 = jnp.concatenate([dm, dm], axis=1)
    prod = dm.astype(F32) * mixf[g, :, mine]
    line = lax.broadcasted_iota(jnp.int32, (16, 2 * SLOT), 0)
    rest = jnp.zeros((WIDER - 16, 2 * SLOT), BF)
    pairs = mask.shape[0]
    kept = [None] * pairs

    def rows_of(p):
        return slice(2 * HEAD_DIM * p, 2 * HEAD_DIM * (p + 1))

    def place_of(p):
        return room.at[pl.ds(p // 3 * 2 * SLOT, 2 * SLOT), pl.ds(p % 3 * 2 * SLOT, 2 * SLOT)]

    def slopes(p):
        mid = 2 * HEAD_DIM * p + HEAD_DIM
        inner = jnp.concatenate(
            [
                jnp.sum(prod[2 * HEAD_DIM * p : mid], axis=0, keepdims=True),
                jnp.sum(prod[mid : mid + HEAD_DIM], axis=0, keepdims=True),
            ],
            axis=1,
        )
        high = inner.astype(BF).astype(F32)
        take_off = jnp.where(line == 0, -high, jnp.where(line == 1, high - inner, 0.0)).astype(BF)
        rhs = dm2 * mask[p, :width, :]
        d_probs = nn(vals, jnp.concatenate([rhs, take_off, rest], axis=0))
        place_of(p)[...] = probs[g, s, p] * d_probs.astype(BF)
        kept[p] = nt(rhs[rows_of(p), :], probs[g, s, p])

    def pull(p):
        head_rows = rows_of(p)
        d_scores = place_of(p)[...]
        dq = pair_rows(nn(keys[head_rows, :], d_scores)) * scale
        dqkv[g, 0, head_rows, mine] = dq.astype(BF)
        qm = (q2 * mask[p, :width, :])[head_rows, :]
        dk = nt(qm, d_scores)
        dv = kept[p]
        dkt[g, head_rows, own] += dk[:, :SLOT]
        dvt[g, head_rows, own] += dv[:, :SLOT]
        dkt[g, head_rows, before] += fprev * dk[:, SLOT:]
        dvt[g, head_rows, before] += fprev * dv[:, SLOT:]
        dkt[g, head_rows, after] += fnext * dk[:, SLOT:]
        dvt[g, head_rows, after] += fnext * dv[:, SLOT:]

    for step in range(pairs + 2):
        if step < pairs:
            slopes(step)
        if step >= 2:
            pull(step - 2)


SQH = 0.7071067811865476
PHI = 0.3989422804014327
MESH = pl.DeviceIdType.MESH
HALVINGS = 3
PIECE = D // 8
LANE = PIECE // 2


class Link:
    def __init__(self, send_sem, recv_sem):
        self.send_sem, self.recv_sem, self.used, self.open = send_sem, recv_sem, 0, []

    def reserve(self, count):
        self.used += count
        return self.used - count

    def make(self, src, dst, target, slot=None):
        slot = self.reserve(1) if slot is None else slot
        return pltpu.make_async_remote_copy(
            src_ref=src, dst_ref=dst, send_sem=self.send_sem.at[slot], recv_sem=self.recv_sem.at[slot],
            device_id=target, device_id_type=MESH,
        )

    def send(self, src, dst, target):
        copy = self.make(src, dst, target)
        copy.start()
        self.open.append(copy)
        return copy

    def done(self, copy):
        copy.wait_send()
        self.open = [c for c in self.open if c is not copy]

    def drain(self):
        for copy in self.open:
            copy.wait_send()
        self.open = []


def add_rows(dst, *terms):
    @pl.loop(0, dst.shape[0] // 16)
    def _(i):
        at = pl.ds(pl.multiple_of(i * 16, 16), 16)
        total = dst[at, :].astype(F32)
        for term in terms:
            total = total + term[at, :].astype(F32)
        dst[at, :] = total.astype(dst.dtype)


def piece_rows(d0, d1, d2, lane):
    return pl.ds(pl.multiple_of(((d0 * 2 + d1) * 2 + d2) * PIECE + lane * LANE, 16), LANE)


class Place:
    def __init__(self, dp_size, shards):
        self.dp = lax.axis_index("dp")
        self.z = lax.axis_index("head")
        self.shards = shards
        self.bits, self.partner = [], []
        step = 1
        while step < dp_size:
            bit = (self.dp // step) % 2
            self.bits.append(bit)
            self.partner.append(self.dp + step - 2 * step * bit)
            step *= 2
        self.order = ((0, 1, 2), (0, 2, 1))

    def near(self, bit):
        return {"dp": self.partner[bit]}

    def across(self, k):
        step, found = 1, 0
        while step < self.shards:
            found = found + step * ((self.z // step + k // step) % 2)
            step *= 2
        return found

    def index(self, lane):
        return tuple(self.bits[b] for b in self.order[lane])


class Halve:
    def __init__(self, link, place, g, r0, r1, r2, rx):
        self.link, self.place, self.g, self.r0, self.r1, self.r2, self.rx = link, place, g, r0, r1, r2, rx

    def start(self):
        p = self.place
        self.pass_on, self.keep = [], []
        for side, out in ((1, self.pass_on), (0, self.keep)):
            for lane in range(2):
                c0, c1, _ = p.index(lane)
                d1 = c1 + side * (1 - 2 * c1)
                out.append(
                    [
                        self.link.send(
                            self.g.at[piece_rows(1 - c0, d1, b, lane)], self.r0.at[piece_rows(0, d1, b, lane)], p.near(0)
                        )
                        for b in range(2)
                    ]
                )

    def mine(self, lane):
        return self.g.at[piece_rows(*self.place.index(lane), lane)]

    def step1(self):
        p = self.place
        self.copies = []
        for lane in range(2):
            c0, c1, _ = p.index(lane)
            sent = []
            for b in range(2):
                self.pass_on[lane][b].wait_recv()
                part = self.g.at[piece_rows(c0, 1 - c1, b, lane)]
                add_rows(part, self.r0.at[piece_rows(0, 1 - c1, b, lane)])
                sent.append(self.link.send(part, self.r1.at[lane, b], p.near(p.order[lane][1])))
            self.copies.append(sent)

    def step2(self):
        p = self.place
        old, self.copies = self.copies, []
        for lane in range(2):
            c0, c1, c2 = p.index(lane)
            for b in range(2):
                self.keep[lane][b].wait_recv()
                old[lane][b].wait_recv()
            part = self.g.at[piece_rows(c0, c1, 1 - c2, lane)]
            add_rows(part, self.r0.at[piece_rows(0, c1, 1 - c2, lane)], self.r1.at[lane, 1 - c2])
            self.copies.append(self.link.send(part, self.r2.at[lane], p.near(p.order[lane][2])))

    def step3(self):
        p = self.place
        for lane in range(2):
            _, c1, c2 = p.index(lane)
            self.copies[lane].wait_recv()
            add_rows(self.mine(lane), self.r0.at[piece_rows(0, c1, c2, lane)], self.r1.at[lane, c2], self.r2.at[lane])
        for extra in range(HALVINGS, len(p.bits)):
            copies = [
                self.link.send(self.mine(lane), self.rx.at[extra - HALVINGS, lane], p.near(extra)) for lane in range(2)
            ]
            for lane in range(2):
                copies[lane].wait_recv()
                self.link.done(copies[lane])
                add_rows(self.mine(lane), self.rx.at[extra - HALVINGS, lane])


class Spread:
    def __init__(self, link, place, f):
        self.link, self.place, self.f = link, place, f

    def swap(self, rows, bit):
        part = self.f.at[rows]
        return self.link.send(part, part, self.place.near(bit))

    def begin(self):
        self.first, self.second, self.core = [], [[], []], []

    def pass_on(self, lane, rows):
        self.second[lane].append(self.swap(rows, self.place.order[lane][1]))
        self.core.append(self.swap(rows, 0))

    def start(self):
        p = self.place
        self.begin()
        for lane in range(2):
            own = piece_rows(*p.index(lane), lane)
            self.first.append(self.swap(own, p.order[lane][2]))
            self.pass_on(lane, own)

    def step1(self):
        p = self.place
        for lane in range(2):
            c0, c1, c2 = p.index(lane)
            self.first[lane].wait_recv()
            self.pass_on(lane, piece_rows(c0, c1, 1 - c2, lane))

    def step2(self):
        p = self.place
        for lane in range(2):
            c0, c1, c2 = p.index(lane)
            for copy in self.second[lane]:
                copy.wait_recv()
            for b in range(2):
                self.core.append(self.swap(piece_rows(c0, 1 - c1, b, lane), 0))

    def finish(self):
        for copy in self.core:
            copy.wait_recv()


def kernel(
    dp_size, shards,
    mol, fill, x, cot_in, gain_a, gain_f, qkv_in, wo_in, wu_in, wd_in,
    out_to, dtok_to, gains_out, up_to, down_to, own_to,
    wg, cot, wu, wd, f_ud, f_own,
    nw, xh, mask, qt, kt, vt, kn, vn, probs, share, mixf, mixt, dmt, dbr, dres,
    dqkv, dkt, dvt, halo_out, halo_in, g_ud, g_k, r0, r1, r2, rx, zud, zk,
    gain_sum, gain_got, gain_col,
    send_sem, recv_sem, halo_send, halo_recv, load_sem,
):
    place = Place(dp_size, shards)
    link = Link(send_sem, recv_sem)
    z = place.z
    last = shards - 1
    nffn, hidden, dinner, out = (g_k.at[i, pl.ds(0, ROWS)] for i in range(4))
    scale = HEAD_DIM ** (-0.5)
    width = dmt.shape[1]

    def column(k):
        return {"head": place.across(k)}

    moves = []

    def move(src, dst):
        copy = pltpu.make_async_copy(src, dst, load_sem.at[len(moves)])
        copy.start()
        moves.append(copy)
        return copy

    own_w = [
        move(qkv_in, wg.at[z, pl.ds(0, 3 * width)]),
        move(wo_in, wg.at[z, pl.ds(3 * width, width)]),
    ]
    ffn_w = [move(wu_in, wu), move(wd_in, wd), move(cot_in, cot)]

    barrier = pltpu.get_barrier_semaphore()
    peers = [place.near(b) for b in range(len(place.bits))] + [column(k) for k in range(1, shards)]
    for peer in peers:
        pl.semaphore_signal(barrier, inc=1, device_id=peer, device_id_type=MESH)
    pl.semaphore_wait(barrier, len(peers))

    after = {"head": jnp.minimum(z + 1, last)}
    before = {"head": jnp.maximum(z - 1, 0)}
    to_next = link.make(x.at[pl.ds(ROWS - SLOT, SLOT)], xh.at[0], after)
    to_prev = link.make(x.at[pl.ds(0, SLOT)], xh.at[1], before)

    for copy in own_w:
        copy.wait()
    lanes = [piece_rows(*place.index(lane), lane) for lane in range(2)]
    inner = (z > 0) & (z < last)
    outer = (z == 0) | (z == last)
    near_z = [place.across(1), 2 - z // 2, last - last * (z // 2)]
    line = link.reserve(max(10, 2 * shards))
    passed = []

    def along(g, target, step):
        return [
            pltpu.make_async_remote_copy(
                src_ref=wg.at[g, rows], dst_ref=wg.at[g, rows],
                send_sem=send_sem.at[line + 2 * step + lane], recv_sem=recv_sem.at[line + 2 * g + lane],
                device_id={"head": target}, device_id_type=MESH,
            )
            for lane, rows in enumerate(lanes)
        ]

    def pass_on(keep, g, target, step):
        copies = along(g, target, step)
        passed.append((keep, copies))

        @pl.when(keep)
        def _():
            for copy in copies:
                copy.start()

    def arrived(g):
        for copy in along(g, after["head"], 0):
            copy.wait_recv()

    pass_on(z < last, z, after["head"], 0)
    pass_on(z > 0, z, before["head"], 1)
    spread = [None] + [Spread(link, place, wg.at[g]) for g in near_z]

    def pick_up(step):
        first, second, third = near_z
        if step == 1:
            arrived(first)
            pass_on(inner, first, last - z, 2)

            @pl.when(inner)
            def _():
                arrived(second)

            pass_on(inner, second, last * (z // 2), 3)
        if step == 2:

            @pl.when(outer)
            def _():
                arrived(second)

            @pl.when(inner)
            def _():
                arrived(third)

            pass_on(inner, third, last * (z // 2), 4)
        if step == 3:

            @pl.when(outer)
            def _():
                arrived(third)

        spread[step].start()

    build_masks(mask, width)
    extend(fill, z, width, qt, kt, vt, kn, vn)

    def normed(at_w, ref, at):
        zz, _ = norm_stats(ref[at, :].astype(F32))
        nw[at_w, :] = (zz * gain_a[...].reshape(1, D)).astype(BF)

    @pl.loop(0, ROWS // 64)
    def _(i):
        at = pl.multiple_of(i * 64, 64)
        normed(pl.ds(at + SLOT, 64), x, pl.ds(at, 64))

    @pl.when(z < last)
    def _():
        to_next.start()

    @pl.when(z > 0)
    def _():
        to_prev.start()

    def weight(g, c):
        return wg[g, c * width : (c + 1) * width, :]

    def heads_mix(g, low, high, step=1):
        @pl.loop(0, (high - low) // step)
        def _(i):
            s = low + i * step
            attend(g, s, slot_meta(mol, z, s), mask, qt, kn, vt, probs, share, mixf, mixt, dkt)

    project(z, [weight(z, c) for c in range(3)], nw, SLOT, ROWS, qt, kt, vt, kn, vn, scale)
    pick_up(1)
    heads_mix(z, 1, SLOTS_DEV - 1)
    spread[1].step1()

    @pl.when(z > 0)
    def _():
        to_next.wait_recv()

    @pl.when(z == 0)
    def _():
        xh[0] = jnp.zeros_like(xh[0])

    @pl.when(z < last)
    def _():
        to_prev.wait_recv()

    @pl.when(z == last)
    def _():
        xh[1] = jnp.zeros_like(xh[1])

    @pl.loop(0, SLOT // 64)
    def _(i):
        at = pl.multiple_of(i * 64, 64)
        normed(pl.ds(at, 64), xh.at[0], pl.ds(at, 64))
        normed(pl.ds(at + SLOT + ROWS, 64), xh.at[1], pl.ds(at, 64))

    for low in (0, SLOT + ROWS):
        project(z, [None, weight(z, 1), weight(z, 2)], nw, low, SLOT, qt, kt, vt, kn, vn, scale)
    pick_up(2)
    spread[1].step2()
    heads_mix(z, 0, 2 * (SLOTS_DEV - 1), SLOTS_DEV - 1)

    def mix_out(g):
        at = pl.ds(pl.multiple_of(g * width, 16), width)
        dres[...] += tn(mixt[at, :], weight(g, 3))

    def heads_in(g):
        project(g, [weight(g, c) for c in range(3)], nw, 0, WIN, qt, kt, vt, kn, vn, scale)

    spread[2].step1()
    pick_up(3)
    dres[...] = x[...].astype(F32)
    mix_out(z)
    for copy in ffn_w:
        copy.wait()
    for i in range(ROWS // SLOT):
        dvt[i, :SLOT, :] = nt(cot[i * SLOT : (i + 1) * SLOT, :], wd[...])
    spread[1].finish()
    heads_in(near_z[0])
    spread[2].step2()
    spread[3].step1()
    heads_mix(near_z[0], 0, SLOTS_DEV)
    mix_out(near_z[0])
    spread[2].finish()
    spread[3].step2()
    heads_in(near_z[1])
    heads_mix(near_z[1], 0, SLOTS_DEV)
    mix_out(near_z[1])
    spread[3].finish()
    heads_in(near_z[2])
    heads_mix(near_z[2], 0, SLOTS_DEV)
    mix_out(near_z[2])

    gain_sum[...] = jnp.zeros_like(gain_sum)
    BLK = 256

    @pl.loop(0, ROWS // BLK)
    def _(i):
        at = pl.ds(pl.multiple_of(i * BLK, BLK), BLK)
        zz, _ = norm_stats(dres[at, :])
        normed_ffn = (zz * gain_f[...].reshape(1, D)).astype(BF)
        nffn[at, :] = normed_ffn
        u = nn(normed_ffn, wu[...])
        dh = jnp.concatenate([dvt[2 * i, :SLOT, :], dvt[2 * i + 1, :SLOT, :]], axis=0)
        cdf = 0.5 + 0.5 * lax.erf(u * SQH)
        h = (u * cdf).astype(BF)
        hidden[at, :] = h
        dinner[at, :] = (dh * (cdf + u * (PHI * jnp.exp(-0.5 * u * u)))).astype(BF)
        out[at, :] = (dres[at, :] + nn(h, wd[...])).astype(BF)

    out_move = move(out, out_to)
    dkt[...] = jnp.zeros_like(dkt)
    dvt[...] = jnp.zeros_like(dvt)
    g_ud[1] = tn(hidden[...], cot[...]).astype(BF)
    down = Halve(link, place, g_ud.at[1], *(r.at[shards + 1] for r in (r0, r1, r2, rx)))
    down.start()
    g_ud[0] = tn(nffn[...], dinner[...]).astype(BF)
    up = Halve(link, place, g_ud.at[0], *(r.at[shards] for r in (r0, r1, r2, rx)))
    up.start()
    down.step1()

    @pl.loop(0, ROWS // BLK)
    def _(i):
        at = pl.ds(pl.multiple_of(i * BLK, BLK), BLK)
        dn = nt(dinner[at, :], wu[...])
        zz, r = norm_stats(dres[at, :])
        gain_sum[1:2, :] += jnp.sum(dn * zz, axis=0, keepdims=True)
        dr = cot[at, :].astype(F32) + norm_back(dn, zz, r, gain_f[...].reshape(1, D))
        dres[at, :] = dr
        dbr[at, :] = dr.astype(BF)

    up.step1()

    def back(g, s):
        attend_back(
            g, s, slot_meta(mol, z, s), mask, qt, kt, vn, dmt, probs, share, mixf, dqkv, dkt, dvt, scale, f_own
        )

    def halo_copy(side, g):
        return pltpu.make_async_remote_copy(
            src_ref=halo_out.at[side, g], dst_ref=halo_in.at[side, g],
            send_sem=halo_send.at[side, g], recv_sem=halo_recv.at[side, g],
            device_id=after if side else before, device_id_type=MESH,
        )

    def border(g):
        dmt[g] = nt(wg[g, 3 * width : 4 * width, :], dbr[...]).astype(BF)

        @pl.loop(0, 2)
        def _(i):
            back(g, i * (SLOTS_DEV - 1))

        for side, cols in ((0, slice(0, SLOT)), (1, slice(SLOT + ROWS, WIN))):
            halo_out[side, g, 0] = dkt[g, :, cols].astype(BF)
            halo_out[side, g, 1] = dvt[g, :, cols].astype(BF)

        @pl.when(z > 0)
        def _():
            halo_copy(0, g).start()

        @pl.when(z < last)
        def _():
            halo_copy(1, g).start()

    def middle(g):
        @pl.loop(1, SLOTS_DEV - 1)
        def _(s):
            back(g, s)

    def shard_grads(k, g):
        @pl.when(z < last)
        def _():
            halo_copy(0, g).wait_recv()
            cols = slice(ROWS, SLOT + ROWS)
            dkt[g, :, cols] += halo_in[0, g, 0].astype(F32)
            dvt[g, :, cols] += halo_in[0, g, 1].astype(F32)

        @pl.when(z > 0)
        def _():
            halo_copy(1, g).wait_recv()
            cols = slice(SLOT, 2 * SLOT)
            dkt[g, :, cols] += halo_in[1, g, 0].astype(F32)
            dvt[g, :, cols] += halo_in[1, g, 1].astype(F32)

        dqkv[g, 1] = dkt[g, :, SLOT : SLOT + ROWS].astype(BF)
        dqkv[g, 2] = dvt[g, :, SLOT : SLOT + ROWS].astype(BF)
        own = nw[SLOT : SLOT + ROWS, :]
        for c in range(3):
            g_k[k, c * width : (c + 1) * width, :] = nn(dqkv[g, c], own).astype(BF)
        at = pl.ds(pl.multiple_of(g * width, 16), width)
        g_k[k, 3 * width : 4 * width, :] = nn(mixt[at, :], dbr[...]).astype(BF)
        job = Halve(link, place, *(r.at[k] for r in (g_k, r0, r1, r2, rx)))
        job.start()
        return job

    def quarter(ref, q):
        lane = q % 2
        c0, ca, cb = place.index(0)
        rows = piece_rows(c0, ca + lane * (cb - ca), cb + lane * (ca - cb), lane)
        return ref.at[rows, pl.ds(pl.multiple_of(q // 2 * (D // 2), 128), D // 2)]

    class Column:
        def __init__(self, i):
            self.g, self.got, self.f, self.spread = g_ud.at[i], zud.at[i], f_ud.at[i], Spread(link, place, f_ud.at[i])

        def send(self):
            self.copies = [
                link.send(quarter(self.g, place.across(k)), self.got.at[k - 1], column(k)) for k in range(1, shards)
            ]

        def sum(self):
            for copy in self.copies:
                copy.wait_recv()
            mine, dst = quarter(self.g, z), quarter(self.f, z)
            add_rows(mine, *[self.got.at[k] for k in range(shards - 1)])
            dst[...] = mine[...]
            self.copies = [link.send(dst, dst, column(k)) for k in range(1, shards)]

        def start(self):
            for copy in self.copies:
                copy.wait_recv()
            self.spread.start()

    up_z, down_z = Column(0), Column(1)
    own_spread = Spread(link, place, f_own)

    def send_shard(k, job):
        return [link.send(job.mine(lane), zk.at[k - 1, lane], column(k)) for lane in range(2)]

    g1, g2, g3 = (place.across(k) for k in (3, 2, 1))
    border(0)
    down.step2()
    border(1)
    up.step2()
    border(2)
    down.step3()
    down_z.send()
    border(3)
    up.step3()
    up_z.send()
    middle(g1)
    down_z.sum()
    job1 = shard_grads(1, g1)
    middle(g2)
    job1.step1()
    up_z.sum()
    job2 = shard_grads(2, g2)
    down_z.start()
    middle(g3)
    job1.step2()
    job2.step1()
    down_z.spread.step1()
    out_move.wait()
    job3 = shard_grads(3, g3)
    up_z.start()
    job1.step3()
    z1 = send_shard(3, job1)
    middle(z)
    job3.step1()
    job2.step2()
    job0 = shard_grads(0, z)
    down_z.spread.step2()
    up_z.spread.step1()

    def tokens_back(low, size):
        at = slice(low, low + size)
        dn = tn(
            dqkv[:, :, :, at].reshape(shards * 3 * width, size),
            jnp.concatenate([wg[g, : 3 * width, :] for g in range(shards)], axis=0),
        )
        zz, r = norm_stats(x[at, :].astype(F32))
        gain_sum[0:1, :] += jnp.sum(dn * zz, axis=0, keepdims=True)
        dres[at, :] = dres[at, :] + norm_back(dn, zz, r, gain_a[...].reshape(1, D))

    tokens_back(0, BLK // 2)
    job0.step1()
    job3.step2()
    job2.step3()
    z2 = send_shard(2, job2)
    tokens_back(BLK // 2, BLK)
    up_z.spread.step2()
    job3.step3()
    z3 = send_shard(1, job3)
    job0.step2()
    tokens_back(BLK // 2 + BLK, BLK // 2)
    move(dres, dtok_to)

    def gain_swap(bit):
        return link.send(gain_sum, gain_got.at[bit], place.near(bit))

    def gain_add(bit, copy):
        copy.wait_recv()
        link.done(copy)
        gain_sum[...] += gain_got[bit]

    swapped = gain_swap(0)
    job0.step3()
    gain_add(0, swapped)
    swapped = gain_swap(1)
    for copy in z1 + z2 + z3:
        copy.wait_recv()
    for lane in range(2):
        mine = job0.mine(lane)
        add_rows(mine, *[zk.at[k, lane] for k in range(shards - 1)])
        f_own.at[piece_rows(*place.index(lane), lane)][...] = mine[...]
    own_spread.start()
    gain_add(1, swapped)
    swapped = gain_swap(2)
    down_z.spread.finish()
    move(f_ud.at[1], down_to)
    own_spread.step1()
    gain_add(2, swapped)
    for bit in range(3, len(place.bits)):
        gain_add(bit, gain_swap(bit))
    gain_col[z] = gain_sum[...]
    gain_copies = [link.send(gain_sum, gain_col.at[z], column(k)) for k in range(1, shards)]
    up_z.spread.finish()
    move(f_ud.at[0], up_to)
    own_spread.step2()
    for copy in gain_copies:
        copy.wait_recv()
    gains_out[...] = sum(gain_col[k] for k in range(shards))
    own_spread.finish()
    move(f_own, own_to)

    link.drain()
    for keep, copies in passed:

        @pl.when(keep)
        def _():
            for copy in copies:
                copy.wait_send()

    @pl.when(z < last)
    def _():
        to_next.wait_send()
        for g in range(shards):
            halo_copy(1, g).wait_send()

    @pl.when(z > 0)
    def _():
        to_prev.wait_send()
        for g in range(shards):
            halo_copy(0, g).wait_send()

    for copy in moves[len(own_w + ffn_w) + 1 :]:
        copy.wait()


VM = pl.BlockSpec(memory_space=pltpu.VMEM)
SM = pl.BlockSpec(memory_space=pltpu.SMEM)
ANY = pl.BlockSpec(memory_space=pl.ANY)
COPIES = 224


def S(shape, dtype):
    return jax.ShapeDtypeStruct(shape, dtype)


def layer(dp_size, n, width, *operands):
    pairs = width // (2 * HEAD_DIM)
    step = 8
    more = 0
    while step < dp_size:
        step *= 2
        more += 1
    extra = max(more, 1)
    bits = 3 + more
    V = pltpu.VMEM
    return pl.pallas_call(
        functools.partial(kernel, dp_size, n),
        out_shape=(
            S((ROWS, D), BF), S((ROWS, D), F32), S((8, D), F32), S((D, D), BF), S((D, D), BF), S((D, D), BF),
        ),
        in_specs=[SM, SM, VM, ANY, VM, VM] + [ANY] * 4,
        out_specs=(ANY, ANY, VM, ANY, ANY, ANY),
        scratch_shapes=[
            V((n, D, D), BF),
            V((ROWS, D), BF),
            V((D, D), BF),
            V((D, D), BF),
            V((2, D, D), BF),
            V((D, D), BF),
            V((WIN, D), BF),
            V((2, SLOT, D), BF),
            V((pairs, width + WIDER, 2 * SLOT), BF),
            V((n, width + WIDER, ROWS), BF),
            V((n, width, WIN), BF),
            V((n, width, WIN), BF),
            V((n, WIN + SLOT, width + WIDER), BF),
            V((n, WIN, width + WIDER), BF),
            V((n, SLOTS_DEV, pairs, 2 * SLOT, 2 * SLOT), BF),
            V((n, width, ROWS), F32),
            V((n, width, ROWS), F32),
            V((D, ROWS), BF),
            V((n, width, ROWS), BF),
            V((ROWS, D), BF),
            V((ROWS, D), F32),
            V((n, 3, width, ROWS), BF),
            V((n, width, WIN), F32),
            V((n, width, WIN), F32),
            V((2, n, 2, width, SLOT), BF),
            V((2, n, 2, width, SLOT), BF),
            V((2, D, D), BF),
            V((n, D, D), BF),
            V((n + 2, D // 2, D), BF),
            V((n + 2, 2, 2, LANE, D), BF),
            V((n + 2, 2, LANE, D), BF),
            V((n + 2, extra, 2, LANE, D), BF),
            V((2, n - 1, LANE, D // 2), BF),
            V((n - 1, 2, LANE, D), BF),
            V((8, D), F32),
            V((bits, 8, D), F32),
            V((n, 8, D), F32),
            pltpu.SemaphoreType.DMA((COPIES + 12 * more,)),
            pltpu.SemaphoreType.DMA((COPIES + 12 * more,)),
            pltpu.SemaphoreType.DMA((2, n)),
            pltpu.SemaphoreType.DMA((2, n)),
            pltpu.SemaphoreType.DMA((16,)),
        ],
        compiler_params=pltpu.CompilerParams(
            vmem_limit_bytes=67043328, collective_id=0, has_side_effects=True
        ),
        name="layer",
    )(*operands)


CHUNK = 128


def finish_kernel(width, out, dtok, gains, up, down, own, *refs):
    outs, (out_v, dtok_v, raw, wide, in_sem, out_sem) = refs[:8], refs[8:]
    out_to, dtok_to, gain_a_to, gain_f_to, qkv_to, wo_to, up_to, down_to = outs
    parts = [(up, up_to, i, i) for i in range(0, D, CHUNK)] + [(down, down_to, i, i) for i in range(0, D, CHUNK)]
    size = CHUNK // 2
    small = [(own, qkv_to, i, i) for i in range(0, 3 * width, size)]
    small += [(own, wo_to, 3 * width + i, i) for i in range(0, width, size)]
    jobs = [(a, b, i, j, CHUNK) for a, b, i, j in parts] + [(a, b, i, j, size) for a, b, i, j in small]
    through = []
    for n, (src, mid, dst) in enumerate(((dtok, dtok_v, dtok_to), (out, out_v, out_to))):
        first = pltpu.make_async_copy(src, mid, in_sem.at[len(jobs) + n])
        first.start()
        through.append((first, pltpu.make_async_copy(mid, dst, out_sem.at[len(jobs) + n])))
    loads, at = [], 0
    for n, (src, _, i, _, rows) in enumerate(jobs):
        copy = pltpu.make_async_copy(src.at[pl.ds(i, rows)], raw.at[pl.ds(at, rows)], in_sem.at[n])
        copy.start()
        loads.append(copy)
        at += rows
    gain_a_to[...] = gains[0, :]
    gain_f_to[...] = gains[1, :]
    stores, at = [], 0
    for first, second in through:
        first.wait()
        second.start()
        stores.append(second)
    for n, (_, dst, _, j, rows) in enumerate(jobs):
        loads[n].wait()

        @pl.loop(0, rows // 16)
        def _(i):
            rows16 = pl.ds(pl.multiple_of(at + i * 16, 16), 16)
            wide[rows16, :] = raw[rows16, :].astype(F32)

        copy = pltpu.make_async_copy(wide.at[pl.ds(at, rows)], dst.at[pl.ds(j, rows)], out_sem.at[n])
        copy.start()
        stores.append(copy)
        at += rows
    for copy in stores:
        copy.wait()


def finish(width, *operands):
    V = pltpu.VMEM
    sems = pltpu.SemaphoreType.DMA((2 * D // CHUNK + 2 * D // CHUNK + 2,))
    return pl.pallas_call(
        functools.partial(finish_kernel, width),
        out_shape=(
            S((ROWS, D), BF), S((ROWS, D), F32), S((D,), F32), S((D,), F32),
            S((3 * width, D), F32), S((width, D), F32), S((D, D), F32), S((D, D), F32),
        ),
        in_specs=[ANY, ANY, VM, ANY, ANY, ANY],
        out_specs=(ANY, ANY, VM, VM, ANY, ANY, ANY, ANY),
        scratch_shapes=[V((ROWS, D), BF), V((ROWS, D), F32), V((3 * D, D), BF), V((3 * D, D), F32), sems, sems],
        name="finish",
    )(*operands)


def local(tokens_in, gain_attn, gain_ffn, w_qkv, w_out, w_up, w_down, slot_mol, slot_fill, cotangent):
    n = lax.axis_size("head")
    width = w_out.shape[0]
    results = layer(
        lax.axis_size("dp"), n, width,
        slot_mol, slot_fill, tokens_in, cotangent, gain_attn, gain_ffn,
        w_qkv.transpose(0, 2, 1).reshape(3 * width, D), w_out, w_up, w_down,
    )
    out, dtok, d_gain_a, d_gain_f, d_qkv, d_wo, d_up, d_down = finish(width, *results)
    return (
        out, dtok, d_gain_a, d_gain_f, d_qkv.reshape(3, width, D).transpose(0, 2, 1), d_wo, d_up, d_down,
    )


def solution(mesh):
    return jax.shard_map(
        local,
        mesh=mesh,
        in_specs=(
            P(("dp", "head"), None), P(), P(), P(None, None, "head"), P("head", None), P(), P(),
            P("dp", None), P("dp", None), P(("dp", "head"), None),
        ),
        out_specs=(
            P(("dp", "head"), None), P(("dp", "head"), None), P(), P(), P(None, None, "head"), P("head", None), P(), P(),
        ),
        check_vma=False,
    )
```
